32 devices in a mesh: groups: 2 (over x), dom: 16 (over z, y, core).
Axes of the slice: x: 2, y: 2, z: 4, core: 2. Of those that a mesh axis runs over, the one named last changes fastest.
Arguments:
- grid: bfloat16 [32768, 1024], P(('groups', 'dom')), parts along dimension 0, may hold values from -6 to 6
- latent_in: bfloat16 [512, 1024], P(('groups', 'dom')), parts along dimension 0, may hold values from -3 to 3
- grid_gain: float32 [1024], replicated, may hold values from 0.5 to 1.5
- node_gain: float32 [1024], replicated, may hold values from 0.5 to 1.5
- dec_gain: float32 [1024], replicated, may hold values from 0.5 to 1.5
- w_q_enc: bfloat16 [1024, 512], replicated
- w_kv_enc: bfloat16 [1024, 1024], replicated, may hold values from -0.1875 to 0.1875
- w_o_enc: bfloat16 [512, 1024], replicated, may hold values from -0.25 to 0.25
- w_q_dec: bfloat16 [1024, 512], replicated
- w_kv_dec: bfloat16 [1024, 1024], replicated, may hold values from -0.1875 to 0.1875
- w_o_dec: bfloat16 [512, 1024], replicated, may hold values from -0.25 to 0.25
- enc_need: int32 [16, 512], P('dom'), may hold values from 0 to 1023
- enc_slot: int32 [32, 256], P(None, 'dom'), may hold values from 0 to 511
- enc_count: int32 [256], P('dom'), may hold values from 1 to 32
- dec_need: int32 [16, 4096], P('dom'), may hold values from 0 to 15
- dec_slot: int32 [4, 16384], P(None, 'dom'), may hold values from 0 to 4095
Outputs:
- latent_out: bfloat16 [512, 1024], P(('groups', 'dom')), parts along dimension 0
- grid_out: bfloat16 [32768, 1024], P(('groups', 'dom')), parts along dimension 0
The draws below stay inside these ranges and needn't reach their ends.
There are 2 independent parts, one for each index of `groups`. The reference program is written for one: setup_inputs(seed, part) draws one part's arguments, and reference() takes and returns one part's arrays. A program takes and returns all parts, laid end to end along the dimension named above; an argument that names none is the same for every part. Nothing has to cross between parts.
Inputs may be any that keep to these rules, and one draw needn't show every extreme that they name: `enc_need`: a grid point's index within its band; entries may repeat. Edges of node n are enc_slot[0..enc_count[n]-1, n]; entries may repeat. `dec_need`: a latent node's index within its window; entries may repeat. `dec_slot`: entries may repeat.
All inputs are finite; a program needn't handle non-finite values.
Results may differ from the reference program's by a relative error of at most 0.02.
The reference program's roundings to bfloat16 on the way count: a program that leaves them out, or rounds other values in their place, can miss the bound.
Values may be sent and summed in bfloat16 or wider, within the bound.
A program may use at most 128 MiB of HBM per device.

```python
import math
import jax
import jax.numpy as jnp
from jax import lax

D = 1024
HEADS = 8
KE = 32
KD = 4
GP_DEV = 1024
NODE_DEV = 16
HH = 512
GRID = 16384
NODES = 256
N_DOM = 16


def query_weight(key):
    values = jax.random.normal(key, (D, HH), jnp.float32) * D ** (-0.5)
    values = values * 1.5
    return values.astype(jnp.bfloat16)


def draw_w_q_enc(key, part):
    return query_weight(jax.random.fold_in(key, 11))


def draw_w_q_dec(key, part):
    return query_weight(jax.random.fold_in(key, 23))


def with_ends(entries, own_key, smallest, largest):
    dims = entries.shape
    place = [jax.random.randint(jax.random.fold_in(own_key, axis), (), 0, dims[axis]) for axis in range(len(dims))]
    entries = entries.at[tuple(place)].set(smallest)
    longest = dims.index(max(dims))
    place[longest] = (place[longest] + 1) % dims[longest]
    return entries.at[tuple(place)].set(largest)


def levels(key, shape, cuts, least, top_value):
    factor_of, own = 1.0, jax.random.fold_in(key, 6)
    for dim, blocks in cuts:
        heights = jnp.exp(jax.random.uniform(jax.random.fold_in(own, dim), (blocks,), jnp.float32, least / len(cuts), top_value / len(cuts)))
        factor_of = factor_of * jnp.repeat(heights, shape[dim] // blocks).reshape([-1 if axis == dim else 1 for axis in range(len(shape))])
    return factor_of


def noise(own_key, shape, scale, reach, pieces=(), kind=jnp.bfloat16):
    array = scale * jax.random.normal(own_key, shape, jnp.float32)
    if pieces:
        array = array * levels(own_key, shape, pieces, -0.22, 0.18)
    return jnp.clip(array, -reach, reach).astype(kind)


def setup_inputs(seed: int = 0, part: int = 0) -> dict:
    keys = jax.random.split(jax.random.key(seed), 17)
    part_splits = jax.random.split(jax.random.fold_in(keys[16], part), 17)
    return {
        "grid": noise(part_splits[0], (GRID, D), 1.0, 6.0, ((0, 16),)),
        "latent_in": noise(part_splits[1], (NODES, D), 0.5, 3.0, ((0, 16),)),
        "grid_gain": jnp.clip(1.0 + 0.1 * jax.random.normal(keys[2], (D,), jnp.float32), 0.5, 1.5),
        "node_gain": jnp.clip(1.0 + 0.1 * jax.random.normal(keys[3], (D,), jnp.float32), 0.5, 1.5),
        "dec_gain": jnp.clip(1.0 + 0.1 * jax.random.normal(keys[4], (D,), jnp.float32), 0.5, 1.5),
        "w_q_enc": draw_w_q_enc(jax.random.fold_in(keys[16], 71), part),
        "w_kv_enc": noise(keys[6], (D, 2 * HH), D ** -0.5, 0.1875),
        "w_o_enc": noise(keys[7], (HH, D), HH ** -0.5, 0.25),
        "w_q_dec": draw_w_q_dec(jax.random.fold_in(keys[16], 71), part),
        "w_kv_dec": noise(keys[9], (D, 2 * HH), D ** -0.5, 0.1875),
        "w_o_dec": noise(keys[10], (HH, D), HH ** -0.5, 0.25),
        "enc_need": with_ends(jax.random.randint(keys[11], (N_DOM, NODE_DEV * KE), 0, GP_DEV), jax.random.fold_in(keys[11], 1), 0, GP_DEV - 1).astype(jnp.int32),
        "enc_slot": with_ends(jax.random.randint(keys[12], (KE, NODES), 0, NODE_DEV * KE), jax.random.fold_in(keys[12], 1), 0, (NODE_DEV * KE) - 1).astype(jnp.int32),
        "enc_count": with_ends(jax.random.randint(keys[13], (NODES,), 1, KE + 1), jax.random.fold_in(keys[13], 1), 1, KE).astype(jnp.int32),
        "dec_need": with_ends(jax.random.randint(keys[14], (N_DOM, GP_DEV * KD), 0, NODE_DEV), jax.random.fold_in(keys[14], 1), 0, NODE_DEV - 1).astype(jnp.int32),
        "dec_slot": with_ends(jax.random.randint(keys[15], (KD, GRID), 0, GP_DEV * KD), jax.random.fold_in(keys[15], 1), 0, (GP_DEV * KD) - 1).astype(jnp.int32),
    }


norm_eps = 1e-06

def rms_norm(values, weight_gain):
    widened = values.astype(jnp.float32)
    spread = lax.optimization_barrier(jnp.mean(widened * widened, axis=-1, keepdims=True))
    return (widened * lax.rsqrt(spread + norm_eps) * weight_gain).astype(jnp.bfloat16)

def attend_keys(queries, key_rows, keep_mask):
    rows_here = queries.shape[0]
    inner_width = queries.shape[1]
    head_size = inner_width // HEADS
    edge_count = key_rows.shape[0]
    query_heads = queries.reshape(rows_here, HEADS, head_size).astype(jnp.float32)
    key_heads = key_rows[..., :inner_width].reshape(edge_count, rows_here, HEADS, head_size).astype(jnp.float32)
    value_heads = key_rows[..., inner_width:].reshape(edge_count, rows_here, HEADS, head_size).astype(jnp.float32)
    scores = jnp.einsum('rhd,krhd->krh', query_heads, key_heads) * (1.0 / math.sqrt(head_size))
    if keep_mask is not None:
        scores = jnp.where(keep_mask[:, :, None], scores, -1e+30)
    highest = lax.optimization_barrier(jnp.max(scores, axis=0, keepdims=True))
    raised = jnp.exp(scores - highest)
    weights = (raised / lax.optimization_barrier(jnp.sum(raised, axis=0, keepdims=True))).astype(jnp.bfloat16)
    mixed = jnp.einsum('krh,krhd->rhd', weights.astype(jnp.float32), value_heads)
    return mixed.reshape(rows_here, inner_width).astype(jnp.bfloat16)

def reference(grid, latent_in, grid_gain, node_gain, dec_gain, w_q_enc, w_kv_enc, w_o_enc, w_q_dec, w_kv_dec, w_o_dec, enc_need, enc_slot, enc_count, dec_need, dec_slot):
    normed_grid = rms_norm(grid, grid_gain)
    grid_pairs = jnp.dot(normed_grid, w_kv_enc, preferred_element_type=jnp.float32).astype(jnp.bfloat16)
    enc_cap = NODE_DEV * KE // N_DOM
    enc_owner = jnp.arange(NODE_DEV * KE, dtype=jnp.int32) // enc_cap

    def encode_block(block):
        wanted = enc_owner * GP_DEV + enc_need[block]
        buffer = grid_pairs[wanted]
        start = (block * NODE_DEV).astype(jnp.int32)
        slots = lax.dynamic_slice_in_dim(enc_slot, start, NODE_DEV, 1)
        counts = lax.dynamic_slice_in_dim(enc_count, start, NODE_DEV, 0)
        own_rows = lax.dynamic_slice_in_dim(latent_in, start, NODE_DEV, 0)
        queries = jnp.dot(rms_norm(own_rows, node_gain), w_q_enc, preferred_element_type=jnp.float32).astype(jnp.bfloat16)
        keep_mask = jnp.arange(KE, dtype=jnp.int32)[:, None] < counts[None, :]
        mixed = attend_keys(queries, buffer[slots], keep_mask)
        update = jnp.dot(mixed, w_o_enc, preferred_element_type=jnp.float32)
        return (own_rows.astype(jnp.float32) + update).astype(jnp.bfloat16)
    latent_out = lax.map(encode_block, jnp.arange(N_DOM, dtype=jnp.int32)).reshape(NODES, D)
    latent_pairs = jnp.dot(rms_norm(latent_out, dec_gain), w_kv_dec, preferred_element_type=jnp.float32).astype(jnp.bfloat16)
    dec_cap = GP_DEV * KD // N_DOM
    dec_owner = jnp.arange(GP_DEV * KD, dtype=jnp.int32) // dec_cap

    def decode_block(block):
        wanted = dec_owner * NODE_DEV + dec_need[block]
        buffer = latent_pairs[wanted]
        start = (block * GP_DEV).astype(jnp.int32)
        slots = lax.dynamic_slice_in_dim(dec_slot, start, GP_DEV, 1)
        own_rows = lax.dynamic_slice_in_dim(grid, start, GP_DEV, 0)
        own_normed = lax.dynamic_slice_in_dim(normed_grid, start, GP_DEV, 0)
        queries = jnp.dot(own_normed, w_q_dec, preferred_element_type=jnp.float32).astype(jnp.bfloat16)
        mixed = attend_keys(queries, buffer[slots], None)
        update = jnp.dot(mixed, w_o_dec, preferred_element_type=jnp.float32)
        return (own_rows.astype(jnp.float32) + update).astype(jnp.bfloat16)
    grid_out = lax.map(decode_block, jnp.arange(N_DOM, dtype=jnp.int32)).reshape(GRID, D)
    return (latent_out, grid_out)
```

```python
import math

import jax
import jax.numpy as jnp
from jax import lax
from jax.sharding import PartitionSpec as P

HEADS = 8
norm_eps = 1e-06
F32 = jnp.float32
BF16 = jnp.bfloat16


def rms_norm(values, weight_gain):
    widened = values.astype(F32)
    spread = jnp.mean(widened * widened, axis=-1, keepdims=True)
    return (widened * lax.rsqrt(spread + norm_eps) * weight_gain).astype(BF16)


def attend_dense(queries, pairs, edges):
    rows, width = queries.shape
    head = width // HEADS
    q = queries.reshape(rows, HEADS, head)
    k = pairs[:, :width].reshape(-1, HEADS, head)
    v = pairs[:, width:].reshape(-1, HEADS, head)
    scores = jnp.einsum("rhd,khd->hrk", q, k, preferred_element_type=F32)
    scores = jnp.where(edges[None] > 0, scores * (1.0 / math.sqrt(head)), -1e30)
    highest = jnp.max(scores, axis=-1, keepdims=True)
    raised = jnp.exp(scores - highest) * edges[None]
    weights = (raised / jnp.sum(raised, axis=-1, keepdims=True)).astype(BF16)
    mixed = jnp.einsum("hrk,khd->rhd", weights, v, preferred_element_type=F32)
    return mixed.reshape(rows, width).astype(BF16)


def on_device(grid, latent_in, grid_gain, node_gain, dec_gain, w_q_enc, w_kv_enc, w_o_enc,
              w_q_dec, w_kv_dec, w_o_dec, enc_need, enc_slot, enc_count, dec_need, dec_slot):
    peers = lax.axis_size("dom")
    nodes = latent_in.shape[0]
    normed_grid = rms_norm(grid, grid_gain)
    wanted = lax.all_to_all(enc_need.reshape(peers, -1), "dom", split_axis=0, concat_axis=0, tiled=True)
    band = jnp.arange(grid.shape[0], dtype=jnp.int32)
    pick = (wanted.reshape(-1)[:, None] == band[None, :]).astype(BF16)
    chosen = jnp.dot(pick, normed_grid, preferred_element_type=F32).astype(BF16)
    rows = jnp.dot(chosen, w_kv_enc, preferred_element_type=F32).astype(BF16)
    arrived = lax.all_to_all(rows, "dom", split_axis=0, concat_axis=0, tiled=True)
    enc_queries = jnp.dot(rms_norm(latent_in, node_gain), w_q_enc, preferred_element_type=F32).astype(BF16)
    live = jnp.arange(enc_slot.shape[0], dtype=jnp.int32)[:, None] < enc_count[None, :]
    slot_row = jnp.arange(enc_need.shape[1], dtype=jnp.int32)
    enc_edges = jnp.sum((live[:, :, None] & (enc_slot[:, :, None] == slot_row)).astype(F32), axis=0)
    enc_mixed = attend_dense(enc_queries, arrived, enc_edges)
    enc_update = jnp.dot(enc_mixed, w_o_enc, preferred_element_type=F32)
    latent_out = (latent_in.astype(F32) + enc_update).astype(BF16)
    latent_pairs = jnp.dot(rms_norm(latent_out, dec_gain), w_kv_dec, preferred_element_type=F32).astype(BF16)
    dec_queries = jnp.dot(normed_grid, w_q_dec, preferred_element_type=F32).astype(BF16)
    everyone = lax.all_gather(latent_pairs, "dom", axis=0, tiled=True)
    total = dec_need.shape[1]
    cap = total // peers
    lanes = 128
    table = dec_need.reshape(total // lanes, lanes).astype(BF16)
    high = (dec_slot // lanes)[:, :, None] == jnp.arange(total // lanes, dtype=jnp.int32)
    low = (dec_slot % lanes)[:, :, None] == jnp.arange(lanes, dtype=jnp.int32)
    need = jnp.einsum("jgt,tl->jgl", high.astype(BF16), table, preferred_element_type=F32)
    need = jnp.sum(jnp.where(low, need, 0.0), axis=-1).astype(jnp.int32)
    node = (dec_slot // cap) * nodes + need
    dec_edges = jnp.sum((node[:, :, None] == jnp.arange(peers * nodes, dtype=jnp.int32)).astype(F32), axis=0)
    dec_mixed = attend_dense(dec_queries, everyone, dec_edges)
    dec_update = jnp.dot(dec_mixed, w_o_dec, preferred_element_type=F32)
    grid_out = (grid.astype(F32) + dec_update).astype(BF16)
    return (latent_out, grid_out)


def solution(mesh):
    both, rep = P(("groups", "dom"), None), P()
    return jax.shard_map(
        on_device,
        mesh=mesh,
        in_specs=(both, both, *([rep] * 9), P("dom", None), P(None, "dom"), P("dom"), P("dom", None), P(None, "dom")),
        out_specs=(both, both),
        check_vma=False,
    )
```

```python
import functools
import math

import jax
import jax.numpy as jnp
from jax import lax
from jax.experimental import pallas as pl
from jax.experimental.pallas import tpu as pltpu
from jax.sharding import PartitionSpec as P

HEADS = 8
norm_eps = 1e-06
F32 = jnp.float32
BF16 = jnp.bfloat16


def rms_norm(values, weight_gain):
    widened = values.astype(F32)
    spread = jnp.mean(widened * widened, axis=-1, keepdims=True)
    return (widened * lax.rsqrt(spread + norm_eps) * weight_gain).astype(BF16)


def attend_dense(queries, pairs, edges):
    rows, width = queries.shape
    head = width // HEADS
    q = queries.reshape(rows, HEADS, head)
    k = pairs[:, :width].reshape(-1, HEADS, head)
    v = pairs[:, width:].reshape(-1, HEADS, head)
    scores = jnp.einsum("rhd,khd->hrk", q, k, preferred_element_type=F32)
    scores = jnp.where(edges[None] > 0, scores * (1.0 / math.sqrt(head)), -1e30)
    highest = jnp.max(scores, axis=-1, keepdims=True)
    raised = jnp.exp(scores - highest) * edges[None]
    weights = (raised / jnp.sum(raised, axis=-1, keepdims=True)).astype(BF16)
    mixed = jnp.einsum("hrk,khd->rhd", weights, v, preferred_element_type=F32)
    return mixed.reshape(rows, width).astype(BF16)


def on_device(grid, latent_in, grid_gain, node_gain, dec_gain, w_q_enc, w_kv_enc, w_o_enc,
              w_q_dec, w_kv_dec, w_o_dec, enc_need, enc_slot, enc_count, dec_need, dec_slot):
    peers = lax.axis_size("dom")
    nodes = latent_in.shape[0]
    normed_grid = rms_norm(grid, grid_gain)
    wanted = lax.all_to_all(enc_need.reshape(peers, -1), "dom", split_axis=0, concat_axis=0, tiled=True)
    band = jnp.arange(grid.shape[0], dtype=jnp.int32)
    pick = (wanted.reshape(-1)[:, None] == band[None, :]).astype(BF16)
    chosen = jnp.dot(pick, normed_grid, preferred_element_type=F32).astype(BF16)
    rows = jnp.dot(chosen, w_kv_enc, preferred_element_type=F32).astype(BF16)
    arrived = lax.all_to_all(rows, "dom", split_axis=0, concat_axis=0, tiled=True)
    enc_queries = jnp.dot(rms_norm(latent_in, node_gain), w_q_enc, preferred_element_type=F32).astype(BF16)
    live = jnp.arange(enc_slot.shape[0], dtype=jnp.int32)[:, None] < enc_count[None, :]
    slot_row = jnp.arange(enc_need.shape[1], dtype=jnp.int32)
    enc_edges = jnp.sum((live[:, :, None] & (enc_slot[:, :, None] == slot_row)).astype(F32), axis=0)
    enc_mixed = attend_dense(enc_queries, arrived, enc_edges)
    enc_update = jnp.dot(enc_mixed, w_o_enc, preferred_element_type=F32)
    latent_out = (latent_in.astype(F32) + enc_update).astype(BF16)
    latent_pairs = jnp.dot(rms_norm(latent_out, dec_gain), w_kv_dec, preferred_element_type=F32).astype(BF16)
    dec_queries = jnp.dot(normed_grid, w_q_dec, preferred_element_type=F32).astype(BF16)
    everyone = lax.all_gather(latent_pairs, "dom", axis=0, tiled=True)
    total = dec_need.shape[1]
    cap = total // peers
    lanes = 128
    table = dec_need.reshape(total // lanes, lanes).astype(BF16)
    high = (dec_slot // lanes)[:, :, None] == jnp.arange(total // lanes, dtype=jnp.int32)
    low = (dec_slot % lanes)[:, :, None] == jnp.arange(lanes, dtype=jnp.int32)
    need = jnp.einsum("jgt,tl->jgl", high.astype(BF16), table, preferred_element_type=F32)
    need = jnp.sum(jnp.where(low, need, 0.0), axis=-1).astype(jnp.int32)
    node = (dec_slot // cap) * nodes + need
    dec_edges = jnp.sum((node[:, :, None] == jnp.arange(peers * nodes, dtype=jnp.int32)).astype(F32), axis=0)
    dec_mixed = attend_dense(dec_queries, everyone, dec_edges)
    dec_update = jnp.dot(dec_mixed, w_o_dec, preferred_element_type=F32)
    grid_out = (grid.astype(F32) + dec_update).astype(BF16)
    return (latent_out, grid_out)


NT = (((1,), (1,)), ((), ()))
TN = (((0,), (0,)), ((), ()))
HIGH = lax.Precision.HIGHEST


def iota(shape, dim):
    return lax.broadcasted_iota(jnp.int32, shape, dim)


def norm_into(values, gain):
    widened = values.astype(F32)
    spread = jnp.mean(widened * widened, axis=-1, keepdims=True)
    return (widened * lax.rsqrt(spread + norm_eps) * gain).astype(BF16)


def encoder_kernel(
    peers, grid_hbm, latent_ref, ggain_ref, ngain_ref, dgain_ref, wq_hbm, wkv_hbm, wo_hbm, wqd_hbm, wkvd_hbm,
    need_ref, slot_ref, count_ref,
    latent_out, pairs_out, queries_out,
    grid_v, wq_v, wkv_v, wo_v, wqd_v, wkvd_v, normed, rows, query_mine, edges_mine,
    need_all, query_all, edges_all, mix_send, stat_send, mix_all, stat_all, pairs_all,
    load_sem, send_sem, recv_sem,
):
    me = lax.axis_index("dom")
    nodes, model = latent_ref.shape
    width = wq_v.shape[1]
    head = width // HEADS
    cap = edges_all.shape[1]
    points = grid_v.shape[0]
    lanes = HEADS * nodes

    loads = [
        pltpu.make_async_copy(source, target, load_sem.at[number])
        for number, (source, target) in enumerate(
            ((wq_hbm, wq_v), (grid_hbm, grid_v), (wkv_hbm, wkv_v), (wqd_hbm, wqd_v), (wo_hbm, wo_v), (wkvd_hbm, wkvd_v))
        )
    ]
    for load in loads:
        load.start()

    barrier = pltpu.get_barrier_semaphore()
    for step in range(1, peers):
        pl.semaphore_signal(
            barrier, inc=1, device_id={"dom": lax.rem(me + step, peers)}, device_id_type=pl.DeviceIdType.MESH
        )

    def message(kind, source, target, to, slot):
        return pltpu.make_async_remote_copy(
            src_ref=source,
            dst_ref=target,
            send_sem=send_sem.at[kind, to],
            recv_sem=recv_sem.at[kind, slot],
            device_id={"dom": to},
            device_id_type=pl.DeviceIdType.MESH,
        )

    def need_to(to, slot):
        return message(0, need_ref, need_all.at[slot], to, slot)

    def query_to(to, slot):
        return message(1, query_mine, query_all.at[slot], to, slot)

    def edges_to(to, slot):
        return message(2, edges_mine.at[to], edges_all.at[slot], to, slot)

    def mix_to(to, slot):
        return message(3, mix_send.at[to], mix_all.at[slot], to, slot)

    def stat_to(to, slot):
        return message(4, stat_send.at[to], stat_all.at[slot], to, slot)

    def pairs_to(to, slot):
        return message(5, pairs_all.at[me], pairs_all.at[slot], to, slot)

    def each_peer(act):
        def body(step, carry):
            act(lax.rem(me + step, peers))
            return carry

        lax.fori_loop(1, peers, body, 0)

    pl.semaphore_wait(barrier, peers - 1)
    each_peer(lambda to: need_to(to, me).start())
    need_all[me] = need_ref[...]

    loads[0].wait()
    queries = jnp.dot(
        norm_into(latent_ref[...], ngain_ref[...]), wq_v[...], preferred_element_type=F32
    ).astype(BF16)
    query_mine[...] = queries
    query_all[me] = queries
    each_peer(lambda to: query_to(to, me).start())

    edge_total = slot_ref.shape[0]
    slots = jnp.where(iota(slot_ref.shape, 0) < count_ref[...], slot_ref[...], -1).astype(F32)
    turn = (iota((edge_total, edge_total), 0) == iota((edge_total, edge_total), 1)).astype(F32)
    by_node = lax.dot_general(slots, turn, TN, precision=HIGH, preferred_element_type=F32)
    entry = iota((nodes, peers * cap), 1).astype(F32)
    tally = jnp.zeros((nodes, peers * cap), F32)
    for j in range(edge_total):
        tally = tally + jnp.where(by_node[:, j : j + 1] == entry, 1.0, 0.0)
    spread_out = (iota((nodes, lanes), 0) == lax.rem(iota((nodes, lanes), 1), nodes)).astype(BF16)
    tally = lax.dot_general(tally.astype(BF16), spread_out, TN, preferred_element_type=F32)
    edges_mine[...] = tally.astype(BF16).reshape(peers, cap, lanes)
    edges_all[me] = edges_mine[me]
    each_peer(lambda to: edges_to(to, me).start())

    loads[1].wait()

    def norm_block(block, carry):
        at = pl.ds(pl.multiple_of(block * 128, 128), 128)
        normed[at, :] = norm_into(grid_v[at, :], ggain_ref[...])
        return carry

    lax.fori_loop(0, points // 128, norm_block, 0)

    each_peer(lambda peer: need_to(peer, peer).wait_recv())
    lists = need_all[...]
    asked = jnp.broadcast_to(lists, (peers, cap, peers * cap))
    mine = iota((peers, cap, peers * cap), 2) == me * cap + iota((peers, cap, peers * cap), 1)
    wanted = jnp.sum(jnp.where(mine, asked.astype(F32), 0.0), axis=2, keepdims=True).astype(jnp.int32)
    wanted = wanted.reshape(peers * cap, 1)
    pick = jnp.where(wanted == iota((peers * cap, points), 1), 1.0, 0.0).astype(BF16)
    chosen = jnp.dot(pick, normed[...], preferred_element_type=F32).astype(BF16)
    loads[2].wait()
    rows[...] = jnp.dot(chosen, wkv_v[...], preferred_element_type=F32).astype(BF16)

    own_head = iota((lanes, width), 0) // nodes == iota((lanes, width), 1) // head

    def window(w):
        spread_query = jnp.broadcast_to(query_all[w][None], (HEADS, nodes, width)).reshape(lanes, width)
        spread_query = jnp.where(own_head, spread_query, jnp.zeros_like(spread_query))
        here = pl.ds(pl.multiple_of(w * cap, cap), cap)
        scores = lax.dot_general(rows[here, :width], spread_query, NT, preferred_element_type=F32)
        times = edges_all[w].astype(F32)
        scores = jnp.where(times > 0, scores * (1.0 / math.sqrt(head)), -1e30)
        highest = jnp.max(scores, axis=0, keepdims=True)
        raised = jnp.exp(scores - highest) * times
        total = jnp.sum(raised, axis=0, keepdims=True)
        mixed = lax.dot_general(raised.astype(BF16), rows[here, width:], TN, preferred_element_type=F32)
        mixed = jnp.where(own_head, mixed, 0.0).reshape(HEADS, nodes, width)
        return jnp.sum(mixed, axis=0).astype(BF16), highest, total

    def serve(peer):
        query_to(peer, peer).wait_recv()
        edges_to(peer, peer).wait_recv()
        mixed, highest, total = window(peer)
        mix_send[peer] = mixed
        stat_send[peer, 0:1, :] = highest
        stat_send[peer, 1:2, :] = total
        mix_to(peer, me).start()
        stat_to(peer, me).start()

    each_peer(serve)
    mixed, highest, total = window(me)
    mix_all[me] = mixed
    stat_all[me, 0:1, :] = highest
    stat_all[me, 1:2, :] = total

    loads[3].wait()
    queries_out[...] = jnp.dot(normed[...], wqd_v[...], preferred_element_type=F32).astype(BF16)

    def take_mix(peer):
        mix_to(peer, peer).wait_recv()
        stat_to(peer, peer).wait_recv()

    each_peer(take_mix)
    tops = [stat_all[peer, 0:1, :] for peer in range(peers)]
    sums = [stat_all[peer, 1:2, :] for peer in range(peers)]
    top = functools.reduce(jnp.maximum, tops)
    shares = [jnp.exp(one - top) for one in tops]
    whole = functools.reduce(jnp.add, [a * b for a, b in zip(shares, sums)])
    own_node = iota((nodes, lanes), 0) == lax.rem(iota((nodes, lanes), 1), nodes)
    stacked = jnp.concatenate([jnp.where(own_node, share / whole, 0.0) for share in shares], axis=0)
    widen = (iota((lanes, width), 0) // nodes == iota((lanes, width), 1) // head).astype(F32)
    factors = jnp.dot(stacked, widen, precision=HIGH, preferred_element_type=F32).reshape(peers, nodes, width)
    enc_mixed = jnp.sum(factors * mix_all[...].astype(F32), axis=0).astype(BF16)
    loads[4].wait()
    update = jnp.dot(enc_mixed, wo_v[...], preferred_element_type=F32)
    fresh = (latent_ref[...].astype(F32) + update).astype(BF16)
    latent_out[...] = fresh
    loads[5].wait()
    pairs = jnp.dot(norm_into(fresh, dgain_ref[...]), wkvd_v[...], preferred_element_type=F32).astype(BF16)
    pairs_all[me] = pairs
    each_peer(lambda to: pairs_to(to, me).start())
    each_peer(lambda peer: pairs_to(peer, peer).wait_recv())
    pairs_out[...] = pairs_all[...].reshape(peers * nodes, model)

    def drain(to):
        for outgoing in (need_to, query_to, edges_to, mix_to, stat_to, pairs_to):
            outgoing(to, me).wait_send()

    each_peer(drain)


def encode(grid, latent_in, grid_gain, node_gain, dec_gain, w_q_enc, w_kv_enc, w_o_enc, w_q_dec, w_kv_dec,
           enc_need, enc_slot, enc_count):
    peers = lax.axis_size("dom")
    nodes, model = latent_in.shape
    width = w_q_enc.shape[1]
    entries = enc_need.shape[1]
    cap = entries // peers
    points = grid.shape[0]
    vmem = pl.BlockSpec(memory_space=pltpu.VMEM)
    far = pl.BlockSpec(memory_space=pl.ANY)
    return pl.pallas_call(
        functools.partial(encoder_kernel, peers),
        name="encode",
        out_shape=(
            jax.ShapeDtypeStruct((nodes, model), BF16),
            jax.ShapeDtypeStruct((peers * nodes, 2 * width), BF16),
            jax.ShapeDtypeStruct((points, width), BF16),
        ),
        in_specs=[far, vmem, vmem, vmem, vmem, far, far, far, far, far, vmem, vmem, vmem],
        out_specs=(vmem, vmem, vmem),
        scratch_shapes=[
            pltpu.VMEM(grid.shape, BF16),
            pltpu.VMEM(w_q_enc.shape, BF16),
            pltpu.VMEM(w_kv_enc.shape, BF16),
            pltpu.VMEM(w_o_enc.shape, BF16),
            pltpu.VMEM(w_q_dec.shape, BF16),
            pltpu.VMEM(w_kv_dec.shape, BF16),
            pltpu.VMEM(grid.shape, BF16),
            pltpu.VMEM((entries, 2 * width), BF16),
            pltpu.VMEM((nodes, width), BF16),
            pltpu.VMEM((peers, cap, HEADS * nodes), BF16),
            pltpu.VMEM((peers, 1, entries), jnp.int32),
            pltpu.VMEM((peers, nodes, width), BF16),
            pltpu.VMEM((peers, cap, HEADS * nodes), BF16),
            pltpu.VMEM((peers, nodes, width), BF16),
            pltpu.VMEM((peers, 2, HEADS * nodes), F32),
            pltpu.VMEM((peers, nodes, width), BF16),
            pltpu.VMEM((peers, 2, HEADS * nodes), F32),
            pltpu.VMEM((peers, nodes, 2 * width), BF16),
            pltpu.SemaphoreType.DMA((6,)),
            pltpu.SemaphoreType.DMA((6, peers)),
            pltpu.SemaphoreType.DMA((6, peers)),
        ],
        compiler_params=pltpu.CompilerParams(
            collective_id=0, has_side_effects=True, vmem_limit_bytes=60 * 1024 * 1024
        ),
    )(grid, latent_in, grid_gain[None], node_gain[None], dec_gain[None], w_q_enc, w_kv_enc, w_o_enc, w_q_dec,
      w_kv_dec, enc_need, enc_slot, enc_count[None])


def decoder_kernel(cap, nodes, query_ref, pairs_ref, slot_ref, table_ref, grid_ref, wo_ref, out_ref, turned, mixed):
    tile, width = query_ref.shape
    head = width // HEADS
    keys = pairs_ref.shape[0]

    @pl.when(pl.program_id(0) == 0)
    def _():
        turned[...] = pairs_ref[:, width:].astype(F32).T.astype(BF16)

    slots = slot_ref[...]
    edge_total = slots.shape[0]
    slots = jnp.concatenate([slots] * (8 // edge_total), axis=0)
    columns = []
    for part in range(tile // 128):
        piece = slots[:, part * 128 : (part + 1) * 128]
        high = piece // 128
        low = lax.rem(piece, 128)
        need = jnp.zeros_like(piece)
        for line in range(table_ref.shape[0]):
            entry = jnp.broadcast_to(table_ref[line : line + 1, :], piece.shape)
            need = jnp.where(high == line, jnp.take_along_axis(entry, low, axis=1), need)
        columns.append((piece // cap) * nodes + need)
    node = jnp.concatenate(columns, axis=1)
    name = iota((keys, tile), 0)
    times = jnp.zeros((keys, tile), F32)
    for j in range(edge_total):
        times = times + jnp.where(node[j : j + 1, :] == name, 1.0, 0.0)
    bias = jnp.where(times > 0, jnp.log(jnp.maximum(times, 1.0)), -1e30)
    lanes_of = iota((keys, 2 * head), 1) // head
    for pair in range(HEADS // 2):
        at = slice(pair * 2 * head, (pair + 1) * 2 * head)
        query = query_ref[:, at]
        key = pairs_ref[:, at] * (1.0 / math.sqrt(head))
        for side in range(2):
            h = pair * 2 + side
            own = jnp.where(lanes_of == side, key, jnp.zeros_like(key))
            scores = lax.dot_general(own, query, NT, preferred_element_type=F32) + bias
            highest = jnp.max(scores, axis=0, keepdims=True)
            raised = jnp.exp(scores - highest)
            total = jnp.sum(raised, axis=0, keepdims=True)
            got = jnp.dot(turned[h * head : (h + 1) * head, :], raised.astype(BF16), preferred_element_type=F32)
            mixed[h * head : (h + 1) * head, :] = (got / total).astype(BF16)
    update = lax.dot_general(mixed[...], wo_ref[...], TN, preferred_element_type=F32)
    out_ref[...] = (grid_ref[...].astype(F32) + update).astype(BF16)


def decode(queries, pairs, dec_slot, dec_need, grid, w_o_dec, nodes):
    peers = lax.axis_size("dom")
    points, model = grid.shape
    width = queries.shape[1]
    tile = 256
    table = dec_need.reshape(-1, 128)
    whole = lambda shape: pl.BlockSpec(shape, lambda i: (0, 0))
    return pl.pallas_call(
        functools.partial(decoder_kernel, dec_need.shape[1] // peers, nodes),
        name="decode",
        grid=(points // tile,),
        out_shape=jax.ShapeDtypeStruct(grid.shape, BF16),
        in_specs=[
            pl.BlockSpec((tile, width), lambda i: (i, 0)),
            whole(pairs.shape),
            pl.BlockSpec((dec_slot.shape[0], tile), lambda i: (0, i)),
            whole(table.shape),
            pl.BlockSpec((tile, model), lambda i: (i, 0)),
            whole(w_o_dec.shape),
        ],
        out_specs=pl.BlockSpec((tile, model), lambda i: (i, 0)),
        scratch_shapes=[pltpu.VMEM((width, pairs.shape[0]), BF16), pltpu.VMEM((width, tile), BF16)],
    )(queries, pairs, dec_slot, table, grid, w_o_dec)


def by_kernels(grid, latent_in, grid_gain, node_gain, dec_gain, w_q_enc, w_kv_enc, w_o_enc,
               w_q_dec, w_kv_dec, w_o_dec, enc_need, enc_slot, enc_count, dec_need, dec_slot):
    latent_out, pairs, queries = encode(
        grid, latent_in, grid_gain, node_gain, dec_gain, w_q_enc, w_kv_enc, w_o_enc, w_q_dec, w_kv_dec,
        enc_need, enc_slot, enc_count)
    grid_out = decode(queries, pairs, dec_slot, dec_need, grid, w_o_dec, latent_in.shape[0])
    return (latent_out, grid_out)


def chosen_form(*args):
    grid, latent_in, enc_need, dec_slot = args[0], args[1], args[11], args[15]
    peers = lax.axis_size("dom")
    cap = enc_need.shape[1] // peers
    small = latent_in.shape[0] * peers <= 256
    fits = cap % 32 == 0 and HEADS * latent_in.shape[0] == 128 and grid.shape[0] % 256 == 0
    if small and fits and 8 % dec_slot.shape[0] == 0:
        return by_kernels(*args)
    return on_device(*args)


def solution(mesh):
    both, rep = P(("groups", "dom"), None), P()
    return jax.shard_map(
        chosen_form,
        mesh=mesh,
        in_specs=(both, both, *([rep] * 9), P("dom", None), P(None, "dom"), P("dom"), P("dom", None), P(None, "dom")),
        out_specs=(both, both),
        check_vma=False,
    )
```

```python
import functools
import math

import jax
import jax.numpy as jnp
from jax import lax
from jax.experimental import pallas as pl
from jax.experimental.pallas import tpu as pltpu
from jax.sharding import PartitionSpec as P

HEADS = 8
norm_eps = 1e-06
F32 = jnp.float32
BF16 = jnp.bfloat16


def rms_norm(values, weight_gain):
    widened = values.astype(F32)
    spread = jnp.mean(widened * widened, axis=-1, keepdims=True)
    return (widened * lax.rsqrt(spread + norm_eps) * weight_gain).astype(BF16)


def attend_dense(queries, pairs, edges):
    rows, width = queries.shape
    head = width // HEADS
    q = queries.reshape(rows, HEADS, head)
    k = pairs[:, :width].reshape(-1, HEADS, head)
    v = pairs[:, width:].reshape(-1, HEADS, head)
    scores = jnp.einsum("rhd,khd->hrk", q, k, preferred_element_type=F32)
    scores = jnp.where(edges[None] > 0, scores * (1.0 / math.sqrt(head)), -1e30)
    highest = jnp.max(scores, axis=-1, keepdims=True)
    raised = jnp.exp(scores - highest) * edges[None]
    weights = (raised / jnp.sum(raised, axis=-1, keepdims=True)).astype(BF16)
    mixed = jnp.einsum("hrk,khd->rhd", weights, v, preferred_element_type=F32)
    return mixed.reshape(rows, width).astype(BF16)


def on_device(grid, latent_in, grid_gain, node_gain, dec_gain, w_q_enc, w_kv_enc, w_o_enc,
              w_q_dec, w_kv_dec, w_o_dec, enc_need, enc_slot, enc_count, dec_need, dec_slot):
    peers = lax.axis_size("dom")
    nodes = latent_in.shape[0]
    normed_grid = rms_norm(grid, grid_gain)
    wanted = lax.all_to_all(enc_need.reshape(peers, -1), "dom", split_axis=0, concat_axis=0, tiled=True)
    band = jnp.arange(grid.shape[0], dtype=jnp.int32)
    pick = (wanted.reshape(-1)[:, None] == band[None, :]).astype(BF16)
    chosen = jnp.dot(pick, normed_grid, preferred_element_type=F32).astype(BF16)
    rows = jnp.dot(chosen, w_kv_enc, preferred_element_type=F32).astype(BF16)
    arrived = lax.all_to_all(rows, "dom", split_axis=0, concat_axis=0, tiled=True)
    enc_queries = jnp.dot(rms_norm(latent_in, node_gain), w_q_enc, preferred_element_type=F32).astype(BF16)
    live = jnp.arange(enc_slot.shape[0], dtype=jnp.int32)[:, None] < enc_count[None, :]
    slot_row = jnp.arange(enc_need.shape[1], dtype=jnp.int32)
    enc_edges = jnp.sum((live[:, :, None] & (enc_slot[:, :, None] == slot_row)).astype(F32), axis=0)
    enc_mixed = attend_dense(enc_queries, arrived, enc_edges)
    enc_update = jnp.dot(enc_mixed, w_o_enc, preferred_element_type=F32)
    latent_out = (latent_in.astype(F32) + enc_update).astype(BF16)
    latent_pairs = jnp.dot(rms_norm(latent_out, dec_gain), w_kv_dec, preferred_element_type=F32).astype(BF16)
    dec_queries = jnp.dot(normed_grid, w_q_dec, preferred_element_type=F32).astype(BF16)
    everyone = lax.all_gather(latent_pairs, "dom", axis=0, tiled=True)
    total = dec_need.shape[1]
    cap = total // peers
    lanes = 128
    table = dec_need.reshape(total // lanes, lanes).astype(BF16)
    high = (dec_slot // lanes)[:, :, None] == jnp.arange(total // lanes, dtype=jnp.int32)
    low = (dec_slot % lanes)[:, :, None] == jnp.arange(lanes, dtype=jnp.int32)
    need = jnp.einsum("jgt,tl->jgl", high.astype(BF16), table, preferred_element_type=F32)
    need = jnp.sum(jnp.where(low, need, 0.0), axis=-1).astype(jnp.int32)
    node = (dec_slot // cap) * nodes + need
    dec_edges = jnp.sum((node[:, :, None] == jnp.arange(peers * nodes, dtype=jnp.int32)).astype(F32), axis=0)
    dec_mixed = attend_dense(dec_queries, everyone, dec_edges)
    dec_update = jnp.dot(dec_mixed, w_o_dec, preferred_element_type=F32)
    grid_out = (grid.astype(F32) + dec_update).astype(BF16)
    return (latent_out, grid_out)


NT = (((1,), (1,)), ((), ()))
TN = (((0,), (0,)), ((), ()))
HIGH = lax.Precision.HIGHEST


def iota(shape, dim):
    return lax.broadcasted_iota(jnp.int32, shape, dim)


def norm_into(values, gain):
    widened = values.astype(F32)
    spread = jnp.mean(widened * widened, axis=-1, keepdims=True)
    return (widened * lax.rsqrt(spread + norm_eps) * gain).astype(BF16)


def encoder_kernel(
    peers, grid_hbm, latent_ref, ggain_ref, ngain_ref, dgain_ref, wq_hbm, wkv_hbm, wo_hbm, wqd_hbm, wkvd_hbm,
    need_ref, slot_ref, count_ref,
    latent_out, pairs_out, queries_out,
    grid_v, wq_v, wkv_v, wo_v, wqd_v, wkvd_v, normed, rows, query_mine, edges_mine,
    need_all, query_all, edges_all, times_all, mix_send, stat_send, mix_all, stat_all, pairs_all,
    load_sem, send_sem, recv_sem,
):
    me = lax.axis_index("dom")
    nodes, model = latent_ref.shape
    width = wq_v.shape[1]
    head = width // HEADS
    cap = need_ref.shape[1] // peers
    group = 128 // cap
    chips = peers // 2
    side = lax.rem(me, 2)
    partner = me + 1 - 2 * side
    points = grid_v.shape[0]
    lanes = HEADS * nodes

    loads = [
        pltpu.make_async_copy(source, target, load_sem.at[number])
        for number, (source, target) in enumerate(
            ((wq_hbm, wq_v), (grid_hbm, grid_v), (wkv_hbm, wkv_v), (wqd_hbm, wqd_v), (wo_hbm, wo_v), (wkvd_hbm, wkvd_v))
        )
    ]
    for load in loads:
        load.start()

    barrier = pltpu.get_barrier_semaphore()
    for step in range(1, peers):
        pl.semaphore_signal(
            barrier, inc=1, device_id={"dom": lax.rem(me + step, peers)}, device_id_type=pl.DeviceIdType.MESH
        )

    def message(kind, source, target, to, slot, way=None):
        return pltpu.make_async_remote_copy(
            src_ref=source,
            dst_ref=target,
            send_sem=send_sem.at[kind, to if way is None else way],
            recv_sem=recv_sem.at[kind, slot],
            device_id={"dom": to},
            device_id_type=pl.DeviceIdType.MESH,
        )

    def need_to(to, slot):
        return message(0, need_ref, need_all.at[slot], to, slot)

    def query_to(to, slot):
        return message(1, query_mine, query_all.at[slot], to, slot)

    def query_on(owner, slot):
        return message(6, query_all.at[owner], query_all.at[slot], partner, slot, owner)

    def pairs_on(owner, slot):
        return message(7, pairs_all.at[owner], pairs_all.at[slot], partner, slot, owner)

    def edges_to(to, slot):
        return message(2, edges_mine.at[to // group], edges_all.at[slot], to, slot)

    def mix_to(to, slot):
        return message(3, mix_send.at[to], mix_all.at[slot], to, slot)

    def stat_to(to, slot):
        return message(4, stat_send.at[to], stat_all.at[slot], to, slot)

    def pairs_to(to, slot):
        return message(5, pairs_all.at[me], pairs_all.at[slot], to, slot)

    def each_peer(act):
        def body(step, carry):
            act(lax.rem(me + step, peers))
            return carry

        lax.fori_loop(1, peers, body, 0)

    def each_chip(act):
        def body(step, carry):
            act(lax.rem(me + 2 * step, peers))
            return carry

        lax.fori_loop(1, chips, body, 0)

    pl.semaphore_wait(barrier, peers - 1)
    each_peer(lambda to: need_to(to, me).start())
    need_all[me] = need_ref[...]

    loads[0].wait()
    queries = jnp.dot(
        norm_into(latent_ref[...], ngain_ref[...]), wq_v[...], preferred_element_type=F32
    ).astype(BF16)
    query_mine[...] = queries
    query_all[me] = queries
    query_to(partner, me).start()
    each_chip(lambda to: query_to(to, me).start())

    edge_total = slot_ref.shape[1]
    slots = jnp.where(iota(slot_ref.shape, 1) < count_ref[...], slot_ref[...], -1)
    entry = iota((nodes, peers * cap), 1)
    tally = jnp.zeros((nodes, peers * cap), F32)
    for j in range(edge_total):
        tally = tally + jnp.where(slots[:, j : j + 1] == entry, 1.0, 0.0)
    tally = tally.astype(BF16)
    for part in range(peers // group):
        edges_mine[part] = tally[:, part * 128 : (part + 1) * 128]
    edges_all[me] = edges_mine[me // group]
    each_peer(lambda to: edges_to(to, me).start())

    loads[1].wait()

    def norm_block(block, carry):
        at = pl.ds(pl.multiple_of(block * 128, 128), 128)
        normed[at, :] = norm_into(grid_v[at, :], ggain_ref[...])
        return carry

    lax.fori_loop(0, points // 128, norm_block, 0)

    each_peer(lambda peer: need_to(peer, peer).wait_recv())
    lists = need_all[...]
    asked = jnp.broadcast_to(lists, (peers, cap, peers * cap))
    mine = iota((peers, cap, peers * cap), 2) == me * cap + iota((peers, cap, peers * cap), 1)
    wanted = jnp.sum(jnp.where(mine, asked.astype(F32), 0.0), axis=2, keepdims=True).astype(jnp.int32)
    wanted = wanted.reshape(peers * cap, 1)
    pick = jnp.where(wanted == iota((peers * cap, points), 1), 1.0, 0.0).astype(BF16)
    chosen = jnp.dot(pick, normed[...], preferred_element_type=F32).astype(BF16)
    loads[2].wait()
    rows[...] = jnp.dot(chosen, wkv_v[...], preferred_element_type=F32).astype(BF16)

    def pass_query(peer):
        query_to(peer, peer).wait_recv()
        query_on(peer, peer).start()

    each_chip(pass_query)
    each_peer(lambda peer: edges_to(peer, peer).wait_recv())
    mine = iota((cap, 128), 1) == lax.rem(me, group) * cap + iota((cap, 128), 0)
    entries = lax.dot_general(
        mine.astype(BF16), edges_all[...].reshape(peers * nodes, 128), NT, preferred_element_type=F32
    ).astype(BF16)
    fan = iota((peers * nodes, peers * lanes), 0)
    fan_lane = iota((peers * nodes, peers * lanes), 1)
    fan = fan == (fan_lane // lanes) * nodes + lax.rem(fan_lane, nodes)
    entries = jnp.dot(entries, jnp.where(fan, 1.0, 0.0).astype(BF16), preferred_element_type=F32)
    for peer in range(peers):
        times_all[peer] = entries[:, peer * lanes : (peer + 1) * lanes]

    own_head = iota((lanes, width), 0) // nodes == iota((lanes, width), 1) // head

    def window(w):
        spread_query = jnp.broadcast_to(query_all[w][None], (HEADS, nodes, width)).reshape(lanes, width)
        spread_query = jnp.where(own_head, spread_query, jnp.zeros_like(spread_query))
        here = pl.ds(pl.multiple_of(w * cap, cap), cap)
        scores = lax.dot_general(rows[here, :width], spread_query, NT, preferred_element_type=F32)
        times = times_all[w]
        scores = jnp.where(times > 0, scores * (1.0 / math.sqrt(head)), -1e30)
        highest = jnp.max(scores, axis=0, keepdims=True)
        raised = jnp.exp(scores - highest) * times
        total = jnp.sum(raised, axis=0, keepdims=True)
        mixed = lax.dot_general(raised.astype(BF16), rows[here, width:], TN, preferred_element_type=F32)
        mixed = jnp.where(own_head, mixed, 0.0).reshape(HEADS, nodes, width)
        return jnp.sum(mixed, axis=0).astype(BF16), highest, total

    def serve(windows):
        for peer, answer in [(peer, window(peer)) for peer in windows]:
            mix_send[peer] = answer[0]
            stat_send[peer, 0:1, :] = answer[1]
            stat_send[peer, 1:2, :] = answer[2]

    def reply(peer):
        mix_to(peer, me).start()
        stat_to(peer, me).start()

    serve([lax.rem(me + 2 * step, peers) for step in range(1, chips)])
    each_chip(reply)
    query_to(partner, partner).wait_recv()

    def take_passed(peer):
        owner = peer + 1 - 2 * side
        query_on(owner, owner).wait_recv()

    each_chip(take_passed)
    serve([lax.rem(partner + 2 * step, peers) for step in range(chips)])
    lax.fori_loop(0, chips, lambda step, carry: (reply(lax.rem(partner + 2 * step, peers)), carry)[1], 0)
    mixed, highest, total = window(me)
    mix_all[me] = mixed
    stat_all[me, 0:1, :] = highest
    stat_all[me, 1:2, :] = total

    loads[3].wait()
    queries_out[...] = jnp.dot(normed[...], wqd_v[...], preferred_element_type=F32).astype(BF16)

    def take_mix(peer):
        mix_to(peer, peer).wait_recv()
        stat_to(peer, peer).wait_recv()

    each_peer(take_mix)
    tops = [stat_all[peer, 0:1, :] for peer in range(peers)]
    sums = [stat_all[peer, 1:2, :] for peer in range(peers)]
    top = functools.reduce(jnp.maximum, tops)
    shares = [jnp.exp(one - top) for one in tops]
    whole = functools.reduce(jnp.add, [a * b for a, b in zip(shares, sums)])
    own_node = iota((nodes, lanes), 0) == lax.rem(iota((nodes, lanes), 1), nodes)
    stacked = jnp.concatenate([jnp.where(own_node, share / whole, 0.0) for share in shares], axis=0)
    widen = (iota((lanes, width), 0) // nodes == iota((lanes, width), 1) // head).astype(F32)
    factors = jnp.dot(stacked, widen, precision=HIGH, preferred_element_type=F32).reshape(peers, nodes, width)
    enc_mixed = jnp.sum(factors * mix_all[...].astype(F32), axis=0).astype(BF16)
    loads[4].wait()
    update = jnp.dot(enc_mixed, wo_v[...], preferred_element_type=F32)
    fresh = (latent_ref[...].astype(F32) + update).astype(BF16)
    latent_out[...] = fresh
    loads[5].wait()
    pairs = jnp.dot(norm_into(fresh, dgain_ref[...]), wkvd_v[...], preferred_element_type=F32).astype(BF16)
    pairs_all[me] = pairs
    each_chip(lambda to: pairs_to(to, me).start())
    pairs_to(partner, me).start()

    def pass_pairs(peer):
        pairs_to(peer, peer).wait_recv()
        pairs_on(peer, peer).start()

    each_chip(pass_pairs)
    pairs_to(partner, partner).wait_recv()

    def take_pairs(peer):
        owner = peer + 1 - 2 * side
        pairs_on(owner, owner).wait_recv()

    each_chip(take_pairs)
    pairs_out[...] = pairs_all[...].reshape(peers * nodes, model)

    def drain(to):
        for outgoing in (need_to, edges_to, mix_to, stat_to):
            outgoing(to, me).wait_send()

    def drain_chip(to):
        query_to(to, me).wait_send()
        pairs_to(to, me).wait_send()
        query_on(to, to).wait_send()
        pairs_on(to, to).wait_send()

    each_peer(drain)
    each_chip(drain_chip)
    query_to(partner, me).wait_send()
    pairs_to(partner, me).wait_send()


def encode(grid, latent_in, grid_gain, node_gain, dec_gain, w_q_enc, w_kv_enc, w_o_enc, w_q_dec, w_kv_dec,
           enc_need, enc_slot, enc_count):
    peers = lax.axis_size("dom")
    nodes, model = latent_in.shape
    width = w_q_enc.shape[1]
    entries = enc_need.shape[1]
    cap = entries // peers
    points = grid.shape[0]
    vmem = pl.BlockSpec(memory_space=pltpu.VMEM)
    far = pl.BlockSpec(memory_space=pl.ANY)
    return pl.pallas_call(
        functools.partial(encoder_kernel, peers),
        name="encode",
        out_shape=(
            jax.ShapeDtypeStruct((nodes, model), BF16),
            jax.ShapeDtypeStruct((peers * nodes, 2 * width), BF16),
            jax.ShapeDtypeStruct((points, width), BF16),
        ),
        in_specs=[far, vmem, vmem, vmem, vmem, far, far, far, far, far, vmem, vmem, vmem],
        out_specs=(vmem, vmem, vmem),
        scratch_shapes=[
            pltpu.VMEM(grid.shape, BF16),
            pltpu.VMEM(w_q_enc.shape, BF16),
            pltpu.VMEM(w_kv_enc.shape, BF16),
            pltpu.VMEM(w_o_enc.shape, BF16),
            pltpu.VMEM(w_q_dec.shape, BF16),
            pltpu.VMEM(w_kv_dec.shape, BF16),
            pltpu.VMEM(grid.shape, BF16),
            pltpu.VMEM((entries, 2 * width), BF16),
            pltpu.VMEM((nodes, width), BF16),
            pltpu.VMEM((entries // 128, nodes, 128), BF16),
            pltpu.VMEM((peers, 1, entries), jnp.int32),
            pltpu.VMEM((peers, nodes, width), BF16),
            pltpu.VMEM((peers, nodes, 128), BF16),
            pltpu.VMEM((peers, cap, HEADS * nodes), F32),
            pltpu.VMEM((peers, nodes, width), BF16),
            pltpu.VMEM((peers, 2, HEADS * nodes), F32),
            pltpu.VMEM((peers, nodes, width), BF16),
            pltpu.VMEM((peers, 2, HEADS * nodes), F32),
            pltpu.VMEM((peers, nodes, 2 * width), BF16),
            pltpu.SemaphoreType.DMA((6,)),
            pltpu.SemaphoreType.DMA((8, peers)),
            pltpu.SemaphoreType.DMA((8, peers)),
        ],
        compiler_params=pltpu.CompilerParams(
            collective_id=0, has_side_effects=True, vmem_limit_bytes=60 * 1024 * 1024
        ),
    )(grid, latent_in, grid_gain[None], node_gain[None], dec_gain[None], w_q_enc, w_kv_enc, w_o_enc, w_q_dec,
      w_kv_dec, enc_need, enc_slot.T, enc_count[:, None])


def decoder_kernel(cap, nodes, query_ref, pairs_ref, slot_ref, table_ref, grid_ref, wo_ref, latent_ref, out_ref, latent_out, keys_of, turned, mixed):
    tile, width = query_ref.shape
    head = width // HEADS
    keys = pairs_ref.shape[0]
    quad = 4

    @pl.when(pl.program_id(0) == 0)
    def _():
        turned[...] = pairs_ref[:, width:].astype(F32).T.astype(BF16)
        latent_out[...] = latent_ref[...]
        lane_head = iota((keys, quad * head), 1) // head
        for h in range(HEADS):
            some = pairs_ref[:, (h // quad) * quad * head : (h // quad + 1) * quad * head] * (1.0 / math.sqrt(head))
            keys_of[h // quad, (h % quad) * keys : (h % quad + 1) * keys, :] = jnp.where(
                lane_head == h % quad, some, jnp.zeros_like(some)
            )

    slots = slot_ref[...]
    edge_total = slots.shape[0]
    slots = jnp.concatenate([slots] * (8 // edge_total), axis=0)
    columns = []
    for part in range(tile // 128):
        piece = slots[:, part * 128 : (part + 1) * 128]
        high = piece // 128
        low = lax.rem(piece, 128)
        need = jnp.zeros_like(piece)
        for line in range(table_ref.shape[0]):
            entry = jnp.broadcast_to(table_ref[line : line + 1, :], piece.shape)
            need = jnp.where(high == line, jnp.take_along_axis(entry, low, axis=1), need)
        columns.append((piece // cap) * nodes + need)
    node = jnp.concatenate(columns, axis=1)
    name = iota((keys, tile), 0)
    times = jnp.zeros((keys, tile), F32)
    for j in range(edge_total):
        times = times + jnp.where(node[j : j + 1, :] == name, 1.0, 0.0)
    bias = jnp.where(times > 0, jnp.log(jnp.maximum(times, 1.0)), -1e30)
    for four in range(HEADS // quad):
        query = query_ref[:, four * quad * head : (four + 1) * quad * head]
        for side in range(quad):
            h = four * quad + side
            own = keys_of[four, side * keys : (side + 1) * keys, :]
            scores = lax.dot_general(own, query, NT, preferred_element_type=F32) + bias
            highest = jnp.max(scores, axis=0, keepdims=True)
            raised = jnp.exp(scores - highest)
            total = jnp.sum(raised, axis=0, keepdims=True)
            got = jnp.dot(turned[h * head : (h + 1) * head, :], raised.astype(BF16), preferred_element_type=F32)
            mixed[h * head : (h + 1) * head, :] = (got / total).astype(BF16)
    update = lax.dot_general(mixed[...], wo_ref[...], TN, preferred_element_type=F32)
    out_ref[...] = (grid_ref[...].astype(F32) + update).astype(BF16)


def decode(queries, pairs, dec_slot, dec_need, grid, w_o_dec, latent_out):
    peers = lax.axis_size("dom")
    points, model = grid.shape
    width = queries.shape[1]
    nodes = latent_out.shape[0]
    tile = 512
    table = dec_need.reshape(-1, 128)
    whole = lambda shape: pl.BlockSpec(shape, lambda i: (0, 0))
    return pl.pallas_call(
        functools.partial(decoder_kernel, dec_need.shape[1] // peers, nodes),
        name="decode",
        grid=(points // tile,),
        out_shape=(
            jax.ShapeDtypeStruct(grid.shape, BF16),
            jax.ShapeDtypeStruct(latent_out.shape, BF16),
        ),
        in_specs=[
            pl.BlockSpec((tile, width), lambda i: (i, 0)),
            whole(pairs.shape),
            pl.BlockSpec((dec_slot.shape[0], tile), lambda i: (0, i)),
            whole(table.shape),
            pl.BlockSpec((tile, model), lambda i: (i, 0)),
            whole(w_o_dec.shape),
            whole(latent_out.shape),
        ],
        out_specs=(pl.BlockSpec((tile, model), lambda i: (i, 0)), whole(latent_out.shape)),
        scratch_shapes=[pltpu.VMEM((2, 4 * pairs.shape[0], width // 2), BF16), pltpu.VMEM((width, pairs.shape[0]), BF16), pltpu.VMEM((width, tile), BF16)],
    )(queries, pairs, dec_slot, table, grid, w_o_dec, latent_out)


def by_kernels(grid, latent_in, grid_gain, node_gain, dec_gain, w_q_enc, w_kv_enc, w_o_enc,
               w_q_dec, w_kv_dec, w_o_dec, enc_need, enc_slot, enc_count, dec_need, dec_slot):
    latent_out, pairs, queries = encode(
        grid, latent_in, grid_gain, node_gain, dec_gain, w_q_enc, w_kv_enc, w_o_enc, w_q_dec, w_kv_dec,
        enc_need, enc_slot, enc_count)
    grid_out, latent_out = decode(queries, pairs, dec_slot, dec_need, grid, w_o_dec, latent_out)
    return (latent_out, grid_out)


def chosen_form(*args):
    grid, latent_in, enc_need, dec_slot = args[0], args[1], args[11], args[15]
    peers = lax.axis_size("dom")
    cap = enc_need.shape[1] // peers
    small = latent_in.shape[0] * peers <= 256
    fits = peers % 2 == 0 and 128 % cap == 0 and cap % 32 == 0 and HEADS * latent_in.shape[0] == 128 and grid.shape[0] % 512 == 0
    if small and fits and 8 % dec_slot.shape[0] == 0:
        return by_kernels(*args)
    return on_device(*args)


def solution(mesh):
    both, rep = P(("groups", "dom"), None), P()
    return jax.shard_map(
        chosen_form,
        mesh=mesh,
        in_specs=(both, both, *([rep] * 9), P("dom", None), P(None, "dom"), P("dom"), P("dom", None), P(None, "dom")),
        out_specs=(both, both),
        check_vma=False,
    )
```

```python
import functools
import math

import jax
import jax.numpy as jnp
from jax import lax
from jax.experimental import pallas as pl
from jax.experimental.pallas import tpu as pltpu
from jax.sharding import PartitionSpec as P

HEADS = 8
norm_eps = 1e-06
F32 = jnp.float32
BF16 = jnp.bfloat16


def rms_norm(values, weight_gain):
    widened = values.astype(F32)
    spread = jnp.mean(widened * widened, axis=-1, keepdims=True)
    return (widened * lax.rsqrt(spread + norm_eps) * weight_gain).astype(BF16)


def attend_dense(queries, pairs, edges):
    rows, width = queries.shape
    head = width // HEADS
    q = queries.reshape(rows, HEADS, head)
    k = pairs[:, :width].reshape(-1, HEADS, head)
    v = pairs[:, width:].reshape(-1, HEADS, head)
    scores = jnp.einsum("rhd,khd->hrk", q, k, preferred_element_type=F32)
    scores = jnp.where(edges[None] > 0, scores * (1.0 / math.sqrt(head)), -1e30)
    highest = jnp.max(scores, axis=-1, keepdims=True)
    raised = jnp.exp(scores - highest) * edges[None]
    weights = (raised / jnp.sum(raised, axis=-1, keepdims=True)).astype(BF16)
    mixed = jnp.einsum("hrk,khd->rhd", weights, v, preferred_element_type=F32)
    return mixed.reshape(rows, width).astype(BF16)


def on_device(grid, latent_in, grid_gain, node_gain, dec_gain, w_q_enc, w_kv_enc, w_o_enc,
              w_q_dec, w_kv_dec, w_o_dec, enc_need, enc_slot, enc_count, dec_need, dec_slot):
    peers = lax.axis_size("dom")
    nodes = latent_in.shape[0]
    normed_grid = rms_norm(grid, grid_gain)
    wanted = lax.all_to_all(enc_need.reshape(peers, -1), "dom", split_axis=0, concat_axis=0, tiled=True)
    band = jnp.arange(grid.shape[0], dtype=jnp.int32)
    pick = (wanted.reshape(-1)[:, None] == band[None, :]).astype(BF16)
    chosen = jnp.dot(pick, normed_grid, preferred_element_type=F32).astype(BF16)
    rows = jnp.dot(chosen, w_kv_enc, preferred_element_type=F32).astype(BF16)
    arrived = lax.all_to_all(rows, "dom", split_axis=0, concat_axis=0, tiled=True)
    enc_queries = jnp.dot(rms_norm(latent_in, node_gain), w_q_enc, preferred_element_type=F32).astype(BF16)
    live = jnp.arange(enc_slot.shape[0], dtype=jnp.int32)[:, None] < enc_count[None, :]
    slot_row = jnp.arange(enc_need.shape[1], dtype=jnp.int32)
    enc_edges = jnp.sum((live[:, :, None] & (enc_slot[:, :, None] == slot_row)).astype(F32), axis=0)
    enc_mixed = attend_dense(enc_queries, arrived, enc_edges)
    enc_update = jnp.dot(enc_mixed, w_o_enc, preferred_element_type=F32)
    latent_out = (latent_in.astype(F32) + enc_update).astype(BF16)
    latent_pairs = jnp.dot(rms_norm(latent_out, dec_gain), w_kv_dec, preferred_element_type=F32).astype(BF16)
    dec_queries = jnp.dot(normed_grid, w_q_dec, preferred_element_type=F32).astype(BF16)
    everyone = lax.all_gather(latent_pairs, "dom", axis=0, tiled=True)
    total = dec_need.shape[1]
    cap = total // peers
    lanes = 128
    table = dec_need.reshape(total // lanes, lanes).astype(BF16)
    high = (dec_slot // lanes)[:, :, None] == jnp.arange(total // lanes, dtype=jnp.int32)
    low = (dec_slot % lanes)[:, :, None] == jnp.arange(lanes, dtype=jnp.int32)
    need = jnp.einsum("jgt,tl->jgl", high.astype(BF16), table, preferred_element_type=F32)
    need = jnp.sum(jnp.where(low, need, 0.0), axis=-1).astype(jnp.int32)
    node = (dec_slot // cap) * nodes + need
    dec_edges = jnp.sum((node[:, :, None] == jnp.arange(peers * nodes, dtype=jnp.int32)).astype(F32), axis=0)
    dec_mixed = attend_dense(dec_queries, everyone, dec_edges)
    dec_update = jnp.dot(dec_mixed, w_o_dec, preferred_element_type=F32)
    grid_out = (grid.astype(F32) + dec_update).astype(BF16)
    return (latent_out, grid_out)


NT = (((1,), (1,)), ((), ()))
TN = (((0,), (0,)), ((), ()))
HIGH = lax.Precision.HIGHEST


def iota(shape, dim):
    return lax.broadcasted_iota(jnp.int32, shape, dim)


def norm_into(values, gain):
    widened = values.astype(F32)
    spread = jnp.mean(widened * widened, axis=-1, keepdims=True)
    return (widened * lax.rsqrt(spread + norm_eps) * gain).astype(BF16)


def encoder_kernel(
    peers, grid_hbm, latent_ref, ggain_ref, ngain_ref, dgain_ref, wq_hbm, wkv_hbm, wo_hbm, wqd_hbm, wkvd_hbm,
    need_ref, slot_ref, count_ref, dslot_ref, table_ref,
    latent_out, pairs_out, queries_out, bias_out,
    grid_v, wq_v, wkv_v, wo_v, wqd_v, wkvd_v, normed, rows, query_mine, edges_mine,
    need_all, query_all, edges_all, times_all, mix_send, stat_send, mix_all, stat_all, pairs_all,
    load_sem, send_sem, recv_sem,
):
    me = lax.axis_index("dom")
    nodes, model = latent_ref.shape
    width = wq_v.shape[1]
    head = width // HEADS
    cap = need_ref.shape[1] // peers
    group = 128 // cap
    chips = peers // 2
    side = lax.rem(me, 2)
    partner = me + 1 - 2 * side
    points = grid_v.shape[0]
    lanes = HEADS * nodes

    loads = [
        pltpu.make_async_copy(source, target, load_sem.at[number])
        for number, (source, target) in enumerate(
            ((wq_hbm, wq_v), (grid_hbm, grid_v), (wkv_hbm, wkv_v), (wqd_hbm, wqd_v), (wo_hbm, wo_v), (wkvd_hbm, wkvd_v))
        )
    ]
    for load in loads:
        load.start()

    barrier = pltpu.get_barrier_semaphore()
    for step in range(1, peers):
        pl.semaphore_signal(
            barrier, inc=1, device_id={"dom": lax.rem(me + step, peers)}, device_id_type=pl.DeviceIdType.MESH
        )

    def message(kind, source, target, to, slot, way=None):
        return pltpu.make_async_remote_copy(
            src_ref=source,
            dst_ref=target,
            send_sem=send_sem.at[kind, to if way is None else way],
            recv_sem=recv_sem.at[kind, slot],
            device_id={"dom": to},
            device_id_type=pl.DeviceIdType.MESH,
        )

    def need_to(to, slot):
        return message(0, need_ref, need_all.at[slot], to, slot)

    def query_to(to, slot):
        return message(1, query_mine, query_all.at[slot], to, slot)

    def query_on(owner, slot):
        return message(6, query_all.at[owner], query_all.at[slot], partner, slot, owner)

    def pairs_on(owner, slot):
        return message(7, pairs_all.at[owner], pairs_all.at[slot], partner, slot, owner)

    def edges_to(to, slot):
        return message(2, edges_mine.at[to // group], edges_all.at[slot], to, slot)

    def mix_to(to, slot):
        return message(3, mix_send.at[to], mix_all.at[slot], to, slot)

    def stat_to(to, slot):
        return message(4, stat_send.at[to], stat_all.at[slot], to, slot)

    def pairs_to(to, slot):
        return message(5, pairs_all.at[me], pairs_all.at[slot], to, slot)

    def each_peer(act):
        def body(step, carry):
            act(lax.rem(me + step, peers))
            return carry

        lax.fori_loop(1, peers, body, 0)

    def each_chip(act):
        def body(step, carry):
            act(lax.rem(me + 2 * step, peers))
            return carry

        lax.fori_loop(1, chips, body, 0)

    edge_total = slot_ref.shape[1]
    own = iota((nodes, nodes), 0) == iota((nodes, nodes), 1)
    counts = jnp.sum(jnp.where(own, count_ref[...].astype(F32), 0.0), axis=1, keepdims=True)
    slots = jnp.where(iota(slot_ref.shape, 1).astype(F32) < counts, slot_ref[...], -1)
    entry = iota((nodes, peers * cap), 1)
    tally = jnp.zeros((nodes, peers * cap), F32)
    for j in range(edge_total):
        tally = tally + jnp.where(slots[:, j : j + 1] == entry, 1.0, 0.0)
    tally = tally.astype(BF16)
    for part in range(peers // group):
        edges_mine[part] = tally[:, part * 128 : (part + 1) * 128]
    edges_all[me] = edges_mine[me // group]
    loads[0].wait()
    queries = jnp.dot(
        norm_into(latent_ref[...], ngain_ref[...]), wq_v[...], preferred_element_type=F32
    ).astype(BF16)
    query_mine[...] = queries
    query_all[me] = queries
    need_all[me] = need_ref[...]

    pl.semaphore_wait(barrier, peers - 1)
    each_peer(lambda to: need_to(to, me).start())
    query_to(partner, me).start()
    each_chip(lambda to: query_to(to, me).start())
    each_peer(lambda to: edges_to(to, me).start())

    loads[1].wait()

    def norm_block(block, carry):
        at = pl.ds(pl.multiple_of(block * 128, 128), 128)
        normed[at, :] = norm_into(grid_v[at, :], ggain_ref[...])
        return carry

    lax.fori_loop(0, points // 128, norm_block, 0)

    each_peer(lambda peer: need_to(peer, peer).wait_recv())
    lists = need_all[...]
    asked = jnp.broadcast_to(lists, (peers, cap, peers * cap))
    mine = iota((peers, cap, peers * cap), 2) == me * cap + iota((peers, cap, peers * cap), 1)
    wanted = jnp.sum(jnp.where(mine, asked.astype(F32), 0.0), axis=2, keepdims=True).astype(jnp.int32)
    wanted = wanted.reshape(peers * cap, 1)
    pick = jnp.where(wanted == iota((peers * cap, points), 1), 1.0, 0.0).astype(BF16)
    chosen = jnp.dot(pick, normed[...], preferred_element_type=F32).astype(BF16)
    def pass_query(peer):
        query_to(peer, peer).wait_recv()
        query_on(peer, peer).start()

    each_chip(pass_query)

    loads[2].wait()
    rows[...] = jnp.dot(chosen, wkv_v[...], preferred_element_type=F32).astype(BF16)

    each_peer(lambda peer: edges_to(peer, peer).wait_recv())
    mine = iota((cap, 128), 1) == lax.rem(me, group) * cap + iota((cap, 128), 0)
    entries = lax.dot_general(
        mine.astype(BF16), edges_all[...].reshape(peers * nodes, 128), NT, preferred_element_type=F32
    ).astype(BF16)
    fan = iota((peers * nodes, peers * lanes), 0)
    fan_lane = iota((peers * nodes, peers * lanes), 1)
    fan = fan == (fan_lane // lanes) * nodes + lax.rem(fan_lane, nodes)
    entries = jnp.dot(entries, jnp.where(fan, 1.0, 0.0).astype(BF16), preferred_element_type=F32)
    for peer in range(peers):
        times_all[peer] = entries[:, peer * lanes : (peer + 1) * lanes]

    own_head = iota((lanes, width), 0) // nodes == iota((lanes, width), 1) // head

    def window(w):
        spread_query = jnp.broadcast_to(query_all[w][None], (HEADS, nodes, width)).reshape(lanes, width)
        spread_query = jnp.where(own_head, spread_query, jnp.zeros_like(spread_query))
        here = pl.ds(pl.multiple_of(w * cap, cap), cap)
        scores = lax.dot_general(rows[here, :width], spread_query, NT, preferred_element_type=F32)
        times = times_all[w]
        scores = jnp.where(times > 0, scores * (1.0 / math.sqrt(head)), -1e30)
        highest = jnp.max(scores, axis=0, keepdims=True)
        raised = jnp.exp(scores - highest) * times
        total = jnp.sum(raised, axis=0, keepdims=True)
        mixed = lax.dot_general(raised.astype(BF16), rows[here, width:], TN, preferred_element_type=F32)
        mixed = jnp.where(own_head, mixed, 0.0).reshape(HEADS, nodes, width)
        return jnp.sum(mixed, axis=0).astype(BF16), highest, total

    def serve(windows):
        for peer, answer in [(peer, window(peer)) for peer in windows]:
            mix_send[peer] = answer[0]
            stat_send[peer, 0:1, :] = answer[1]
            stat_send[peer, 1:2, :] = answer[2]

    def reply(peer):
        mix_to(peer, me).start()
        stat_to(peer, me).start()

    serve([lax.rem(me + 2 * step, peers) for step in range(1, chips)])
    each_chip(reply)
    query_to(partner, partner).wait_recv()

    def take_passed(peer):
        owner = peer + 1 - 2 * side
        query_on(owner, owner).wait_recv()

    each_chip(take_passed)
    serve([lax.rem(partner + 2 * step, peers) for step in range(chips)])
    lax.fori_loop(0, chips, lambda step, carry: (reply(lax.rem(partner + 2 * step, peers)), carry)[1], 0)
    mixed, highest, total = window(me)
    mix_all[me] = mixed
    stat_all[me, 0:1, :] = highest
    stat_all[me, 1:2, :] = total

    loads[3].wait()
    queries_out[...] = jnp.dot(normed[...], wqd_v[...], preferred_element_type=F32).astype(BF16)

    keys = peers * nodes
    dec_cap = table_ref.shape[0] * 128 // peers
    slots = dslot_ref[...]
    edge_total = slots.shape[0]
    slots = jnp.concatenate([slots] * (8 // edge_total), axis=0)
    columns = []
    for part in range(points // 128):
        piece = slots[:, part * 128 : (part + 1) * 128]
        high = piece // 128
        low = lax.rem(piece, 128)
        need = jnp.zeros_like(piece)
        for line in range(table_ref.shape[0]):
            entry = jnp.broadcast_to(table_ref[line : line + 1, :], piece.shape)
            need = jnp.where(high == line, jnp.take_along_axis(entry, low, axis=1), need)
        columns.append((piece // dec_cap) * nodes + need)
    node = jnp.concatenate(columns, axis=1)
    name = iota((keys, points), 0)
    times = jnp.zeros((keys, points), F32)
    for j in range(edge_total):
        times = times + jnp.where(node[j : j + 1, :] == name, 1.0, 0.0)
    bias_out[...] = jnp.where(times > 0, jnp.log(jnp.maximum(times, 1.0)), -1e30)

    def take_mix(peer):
        mix_to(peer, peer).wait_recv()
        stat_to(peer, peer).wait_recv()

    each_peer(take_mix)
    tops = [stat_all[peer, 0:1, :] for peer in range(peers)]
    sums = [stat_all[peer, 1:2, :] for peer in range(peers)]
    top = functools.reduce(jnp.maximum, tops)
    shares = [jnp.exp(one - top) for one in tops]
    whole = functools.reduce(jnp.add, [a * b for a, b in zip(shares, sums)])
    own_node = iota((nodes, lanes), 0) == lax.rem(iota((nodes, lanes), 1), nodes)
    stacked = jnp.concatenate([jnp.where(own_node, share / whole, 0.0) for share in shares], axis=0)
    widen = (iota((lanes, width), 0) // nodes == iota((lanes, width), 1) // head).astype(F32)
    factors = jnp.dot(stacked, widen, precision=HIGH, preferred_element_type=F32).reshape(peers, nodes, width)
    enc_mixed = jnp.sum(factors * mix_all[...].astype(F32), axis=0).astype(BF16)
    loads[4].wait()
    update = jnp.dot(enc_mixed, wo_v[...], preferred_element_type=F32)
    fresh = (latent_ref[...].astype(F32) + update).astype(BF16)
    latent_out[...] = fresh
    loads[5].wait()
    pairs = jnp.dot(norm_into(fresh, dgain_ref[...]), wkvd_v[...], preferred_element_type=F32).astype(BF16)
    pairs_all[me] = pairs
    each_chip(lambda to: pairs_to(to, me).start())
    pairs_to(partner, me).start()

    def pass_pairs(peer):
        pairs_to(peer, peer).wait_recv()
        pairs_on(peer, peer).start()

    each_chip(pass_pairs)
    pairs_to(partner, partner).wait_recv()

    def take_pairs(peer):
        owner = peer + 1 - 2 * side
        pairs_on(owner, owner).wait_recv()

    each_chip(take_pairs)
    pairs_out[...] = pairs_all[...].reshape(peers * nodes, model)

    def drain(to):
        for outgoing in (need_to, edges_to, mix_to, stat_to):
            outgoing(to, me).wait_send()

    def drain_chip(to):
        query_to(to, me).wait_send()
        pairs_to(to, me).wait_send()
        query_on(to, to).wait_send()
        pairs_on(to, to).wait_send()

    each_peer(drain)
    each_chip(drain_chip)
    query_to(partner, me).wait_send()
    pairs_to(partner, me).wait_send()


def encode(grid, latent_in, grid_gain, node_gain, dec_gain, w_q_enc, w_kv_enc, w_o_enc, w_q_dec, w_kv_dec,
           enc_need, enc_slot, enc_count, dec_slot, dec_need):
    peers = lax.axis_size("dom")
    nodes, model = latent_in.shape
    width = w_q_enc.shape[1]
    entries = enc_need.shape[1]
    cap = entries // peers
    points = grid.shape[0]
    vmem = pl.BlockSpec(memory_space=pltpu.VMEM)
    far = pl.BlockSpec(memory_space=pl.ANY)
    return pl.pallas_call(
        functools.partial(encoder_kernel, peers),
        name="encode",
        out_shape=(
            jax.ShapeDtypeStruct((nodes, model), BF16),
            jax.ShapeDtypeStruct((peers * nodes, 2 * width), BF16),
            jax.ShapeDtypeStruct((points, width), BF16),
            jax.ShapeDtypeStruct((peers * nodes, points), F32),
        ),
        in_specs=[far, vmem, vmem, vmem, vmem, far, far, far, far, far, vmem, vmem, vmem, vmem, vmem],
        out_specs=(vmem, vmem, vmem, vmem),
        scratch_shapes=[
            pltpu.VMEM(grid.shape, BF16),
            pltpu.VMEM(w_q_enc.shape, BF16),
            pltpu.VMEM(w_kv_enc.shape, BF16),
            pltpu.VMEM(w_o_enc.shape, BF16),
            pltpu.VMEM(w_q_dec.shape, BF16),
            pltpu.VMEM(w_kv_dec.shape, BF16),
            pltpu.VMEM(grid.shape, BF16),
            pltpu.VMEM((entries, 2 * width), BF16),
            pltpu.VMEM((nodes, width), BF16),
            pltpu.VMEM((entries // 128, nodes, 128), BF16),
            pltpu.VMEM((peers, 1, entries), jnp.int32),
            pltpu.VMEM((peers, nodes, width), BF16),
            pltpu.VMEM((peers, nodes, 128), BF16),
            pltpu.VMEM((peers, cap, HEADS * nodes), F32),
            pltpu.VMEM((peers, nodes, width), BF16),
            pltpu.VMEM((peers, 2, HEADS * nodes), F32),
            pltpu.VMEM((peers, nodes, width), BF16),
            pltpu.VMEM((peers, 2, HEADS * nodes), F32),
            pltpu.VMEM((peers, nodes, 2 * width), BF16),
            pltpu.SemaphoreType.DMA((6,)),
            pltpu.SemaphoreType.DMA((8, peers)),
            pltpu.SemaphoreType.DMA((8, peers)),
        ],
        compiler_params=pltpu.CompilerParams(
            collective_id=0, has_side_effects=True, vmem_limit_bytes=60 * 1024 * 1024
        ),
    )(grid, latent_in, grid_gain[None], node_gain[None], dec_gain[None], w_q_enc, w_kv_enc, w_o_enc, w_q_dec,
      w_kv_dec, enc_need, enc_slot.T, enc_count[None], dec_slot, dec_need.reshape(-1, 128))


def decoder_kernel(query_ref, pairs_ref, bias_ref, grid_ref, wo_ref, latent_ref, out_ref, latent_out, keys_of, turned, mixed):
    tile, width = query_ref.shape
    head = width // HEADS
    keys = pairs_ref.shape[0]
    quad = 4

    @pl.when(pl.program_id(0) == 0)
    def _():
        turned[...] = pairs_ref[:, width:].astype(F32).T.astype(BF16)
        latent_out[...] = latent_ref[...]
        lane_head = iota((keys, quad * head), 1) // head
        for h in range(HEADS):
            some = pairs_ref[:, (h // quad) * quad * head : (h // quad + 1) * quad * head] * (1.0 / math.sqrt(head))
            keys_of[h // quad, (h % quad) * keys : (h % quad + 1) * keys, :] = jnp.where(
                lane_head == h % quad, some, jnp.zeros_like(some)
            )

    for four in range(HEADS // quad):
        query = query_ref[:, four * quad * head : (four + 1) * quad * head]
        for side in range(quad):
            h = four * quad + side
            own = keys_of[four, side * keys : (side + 1) * keys, :]
            scores = lax.dot_general(own, query, NT, preferred_element_type=F32) + bias_ref[...]
            highest = jnp.max(scores, axis=0, keepdims=True)
            raised = jnp.exp(scores - highest)
            total = jnp.sum(raised, axis=0, keepdims=True)
            got = jnp.dot(turned[h * head : (h + 1) * head, :], raised.astype(BF16), preferred_element_type=F32)
            mixed[h * head : (h + 1) * head, :] = (got / total).astype(BF16)
    update = lax.dot_general(mixed[...], wo_ref[...], TN, preferred_element_type=F32)
    out_ref[...] = (grid_ref[...].astype(F32) + update).astype(BF16)


def decode(queries, pairs, bias, grid, w_o_dec, latent_out):
    points, model = grid.shape
    width = queries.shape[1]
    tile = 1024
    whole = lambda shape: pl.BlockSpec(shape, lambda i: (0, 0))
    return pl.pallas_call(
        decoder_kernel,
        name="decode",
        grid=(points // tile,),
        out_shape=(
            jax.ShapeDtypeStruct(grid.shape, BF16),
            jax.ShapeDtypeStruct(latent_out.shape, BF16),
        ),
        in_specs=[
            pl.BlockSpec((tile, width), lambda i: (i, 0)),
            whole(pairs.shape),
            pl.BlockSpec((pairs.shape[0], tile), lambda i: (0, i)),
            pl.BlockSpec((tile, model), lambda i: (i, 0)),
            whole(w_o_dec.shape),
            whole(latent_out.shape),
        ],
        out_specs=(pl.BlockSpec((tile, model), lambda i: (i, 0)), whole(latent_out.shape)),
        scratch_shapes=[pltpu.VMEM((2, 4 * pairs.shape[0], width // 2), BF16), pltpu.VMEM((width, pairs.shape[0]), BF16), pltpu.VMEM((width, tile), BF16)],
    )(queries, pairs, bias, grid, w_o_dec, latent_out)


def by_kernels(grid, latent_in, grid_gain, node_gain, dec_gain, w_q_enc, w_kv_enc, w_o_enc,
               w_q_dec, w_kv_dec, w_o_dec, enc_need, enc_slot, enc_count, dec_need, dec_slot):
    latent_out, pairs, queries, bias = encode(
        grid, latent_in, grid_gain, node_gain, dec_gain, w_q_enc, w_kv_enc, w_o_enc, w_q_dec, w_kv_dec,
        enc_need, enc_slot, enc_count, dec_slot, dec_need)
    grid_out, latent_out = decode(queries, pairs, bias, grid, w_o_dec, latent_out)
    return (latent_out, grid_out)


def chosen_form(*args):
    grid, latent_in, enc_need, dec_slot = args[0], args[1], args[11], args[15]
    peers = lax.axis_size("dom")
    cap = enc_need.shape[1] // peers
    small = latent_in.shape[0] * peers <= 256
    fits = peers % 2 == 0 and 128 % cap == 0 and cap % 32 == 0 and HEADS * latent_in.shape[0] == 128 and grid.shape[0] % 1024 == 0
    if small and fits and 8 % dec_slot.shape[0] == 0:
        return by_kernels(*args)
    return on_device(*args)


def solution(mesh):
    both, rep = P(("groups", "dom"), None), P()
    return jax.shard_map(
        chosen_form,
        mesh=mesh,
        in_specs=(both, both, *([rep] * 9), P("dom", None), P(None, "dom"), P("dom"), P("dom", None), P(None, "dom")),
        out_specs=(both, both),
        check_vma=False,
    )
```

```python
import functools
import math

import jax
import jax.numpy as jnp
from jax import lax
from jax.experimental import pallas as pl
from jax.experimental.pallas import tpu as pltpu
from jax.sharding import PartitionSpec as P

HEADS = 8
norm_eps = 1e-06
F32 = jnp.float32
BF16 = jnp.bfloat16


def rms_norm(values, weight_gain):
    widened = values.astype(F32)
    spread = jnp.mean(widened * widened, axis=-1, keepdims=True)
    return (widened * lax.rsqrt(spread + norm_eps) * weight_gain).astype(BF16)


def attend_dense(queries, pairs, edges):
    rows, width = queries.shape
    head = width // HEADS
    q = queries.reshape(rows, HEADS, head)
    k = pairs[:, :width].reshape(-1, HEADS, head)
    v = pairs[:, width:].reshape(-1, HEADS, head)
    scores = jnp.einsum("rhd,khd->hrk", q, k, preferred_element_type=F32)
    scores = jnp.where(edges[None] > 0, scores * (1.0 / math.sqrt(head)), -1e30)
    highest = jnp.max(scores, axis=-1, keepdims=True)
    raised = jnp.exp(scores - highest) * edges[None]
    weights = (raised / jnp.sum(raised, axis=-1, keepdims=True)).astype(BF16)
    mixed = jnp.einsum("hrk,khd->rhd", weights, v, preferred_element_type=F32)
    return mixed.reshape(rows, width).astype(BF16)


def on_device(grid, latent_in, grid_gain, node_gain, dec_gain, w_q_enc, w_kv_enc, w_o_enc,
              w_q_dec, w_kv_dec, w_o_dec, enc_need, enc_slot, enc_count, dec_need, dec_slot):
    peers = lax.axis_size("dom")
    nodes = latent_in.shape[0]
    normed_grid = rms_norm(grid, grid_gain)
    wanted = lax.all_to_all(enc_need.reshape(peers, -1), "dom", split_axis=0, concat_axis=0, tiled=True)
    band = jnp.arange(grid.shape[0], dtype=jnp.int32)
    pick = (wanted.reshape(-1)[:, None] == band[None, :]).astype(BF16)
    chosen = jnp.dot(pick, normed_grid, preferred_element_type=F32).astype(BF16)
    rows = jnp.dot(chosen, w_kv_enc, preferred_element_type=F32).astype(BF16)
    arrived = lax.all_to_all(rows, "dom", split_axis=0, concat_axis=0, tiled=True)
    enc_queries = jnp.dot(rms_norm(latent_in, node_gain), w_q_enc, preferred_element_type=F32).astype(BF16)
    live = jnp.arange(enc_slot.shape[0], dtype=jnp.int32)[:, None] < enc_count[None, :]
    slot_row = jnp.arange(enc_need.shape[1], dtype=jnp.int32)
    enc_edges = jnp.sum((live[:, :, None] & (enc_slot[:, :, None] == slot_row)).astype(F32), axis=0)
    enc_mixed = attend_dense(enc_queries, arrived, enc_edges)
    enc_update = jnp.dot(enc_mixed, w_o_enc, preferred_element_type=F32)
    latent_out = (latent_in.astype(F32) + enc_update).astype(BF16)
    latent_pairs = jnp.dot(rms_norm(latent_out, dec_gain), w_kv_dec, preferred_element_type=F32).astype(BF16)
    dec_queries = jnp.dot(normed_grid, w_q_dec, preferred_element_type=F32).astype(BF16)
    everyone = lax.all_gather(latent_pairs, "dom", axis=0, tiled=True)
    total = dec_need.shape[1]
    cap = total // peers
    lanes = 128
    table = dec_need.reshape(total // lanes, lanes).astype(BF16)
    high = (dec_slot // lanes)[:, :, None] == jnp.arange(total // lanes, dtype=jnp.int32)
    low = (dec_slot % lanes)[:, :, None] == jnp.arange(lanes, dtype=jnp.int32)
    need = jnp.einsum("jgt,tl->jgl", high.astype(BF16), table, preferred_element_type=F32)
    need = jnp.sum(jnp.where(low, need, 0.0), axis=-1).astype(jnp.int32)
    node = (dec_slot // cap) * nodes + need
    dec_edges = jnp.sum((node[:, :, None] == jnp.arange(peers * nodes, dtype=jnp.int32)).astype(F32), axis=0)
    dec_mixed = attend_dense(dec_queries, everyone, dec_edges)
    dec_update = jnp.dot(dec_mixed, w_o_dec, preferred_element_type=F32)
    grid_out = (grid.astype(F32) + dec_update).astype(BF16)
    return (latent_out, grid_out)


NT = (((1,), (1,)), ((), ()))
TN = (((0,), (0,)), ((), ()))
HIGH = lax.Precision.HIGHEST


def iota(shape, dim):
    return lax.broadcasted_iota(jnp.int32, shape, dim)


def norm_into(values, gain):
    widened = values.astype(F32)
    spread = jnp.mean(widened * widened, axis=-1, keepdims=True)
    return (widened * lax.rsqrt(spread + norm_eps) * gain).astype(BF16)


def encoder_kernel(
    peers, grid_hbm, latent_ref, ggain_ref, ngain_ref, dgain_ref, wq_hbm, wkv_hbm, wo_hbm, wqd_hbm, wkvd_hbm,
    need_ref, slot_ref, count_ref, dslot_ref, table_ref,
    latent_out, pairs_out, queries_hbm, bias_hbm,
    grid_v, wq_v, wkv_v, wo_v, wqd_v, wkvd_v, normed, rows, query_mine, edges_mine,
    need_all, query_all, edges_all, times_all, mix_send, stat_send, mix_all, stat_all, pairs_all,
    queries_out, bias_out, load_sem, store_sem, send_sem, recv_sem,
):
    me = lax.axis_index("dom")
    nodes, model = latent_ref.shape
    width = wq_v.shape[1]
    head = width // HEADS
    cap = need_ref.shape[1] // peers
    group = 128 // cap
    chips = peers // 2
    side = lax.rem(me, 2)
    partner = me + 1 - 2 * side
    points = grid_v.shape[0]
    lanes = HEADS * nodes

    loads = [
        pltpu.make_async_copy(source, target, load_sem.at[number])
        for number, (source, target) in enumerate(
            ((wq_hbm, wq_v), (grid_hbm, grid_v), (wkv_hbm, wkv_v), (wqd_hbm, wqd_v), (wo_hbm, wo_v), (wkvd_hbm, wkvd_v))
        )
    ]
    for load in loads:
        load.start()

    barrier = pltpu.get_barrier_semaphore()
    for step in range(1, peers):
        pl.semaphore_signal(
            barrier, inc=1, device_id={"dom": lax.rem(me + step, peers)}, device_id_type=pl.DeviceIdType.MESH
        )

    def message(kind, source, target, to, slot, way=None):
        return pltpu.make_async_remote_copy(
            src_ref=source,
            dst_ref=target,
            send_sem=send_sem.at[kind, to if way is None else way],
            recv_sem=recv_sem.at[kind, slot],
            device_id={"dom": to},
            device_id_type=pl.DeviceIdType.MESH,
        )

    def need_to(to, slot):
        return message(0, need_ref, need_all.at[slot], to, slot)

    def query_to(to, slot):
        return message(1, query_mine, query_all.at[slot], to, slot)

    def query_on(owner, slot):
        return message(6, query_all.at[owner], query_all.at[slot], partner, slot, owner)

    def pairs_on(owner, slot):
        return message(7, pairs_all.at[owner], pairs_all.at[slot], partner, slot, owner)

    def edges_to(to, slot):
        return message(2, edges_mine.at[to // group], edges_all.at[slot], to, slot)

    def mix_to(to, slot):
        return message(3, mix_send.at[to], mix_all.at[slot], to, slot)

    def stat_to(to, slot):
        return message(4, stat_send.at[to], stat_all.at[slot], to, slot)

    def pairs_to(to, slot):
        return message(5, pairs_all.at[me], pairs_all.at[slot], to, slot)

    def each_peer(act):
        def body(step, carry):
            act(lax.rem(me + step, peers))
            return carry

        lax.fori_loop(1, peers, body, 0)

    def each_chip(act):
        def body(step, carry):
            act(lax.rem(me + 2 * step, peers))
            return carry

        lax.fori_loop(1, chips, body, 0)

    edge_total = slot_ref.shape[1]
    own = iota((nodes, nodes), 0) == iota((nodes, nodes), 1)
    counts = jnp.sum(jnp.where(own, count_ref[...].astype(F32), 0.0), axis=1, keepdims=True)
    slots = jnp.where(iota(slot_ref.shape, 1).astype(F32) < counts, slot_ref[...], -1)
    entry = iota((nodes, peers * cap), 1)
    tally = jnp.zeros((nodes, peers * cap), F32)
    for j in range(edge_total):
        tally = tally + jnp.where(slots[:, j : j + 1] == entry, 1.0, 0.0)
    tally = tally.astype(BF16)
    for part in range(peers // group):
        edges_mine[part] = tally[:, part * 128 : (part + 1) * 128]
    edges_all[me] = edges_mine[me // group]
    loads[0].wait()
    queries = jnp.dot(
        norm_into(latent_ref[...], ngain_ref[...]), wq_v[...], preferred_element_type=F32
    ).astype(BF16)
    query_mine[...] = queries
    query_all[me] = queries
    need_all[me] = need_ref[...]

    pl.semaphore_wait(barrier, peers - 1)
    each_peer(lambda to: need_to(to, me).start())
    query_to(partner, me).start()
    each_chip(lambda to: query_to(to, me).start())
    each_peer(lambda to: edges_to(to, me).start())

    loads[1].wait()

    def norm_block(block, carry):
        at = pl.ds(pl.multiple_of(block * 128, 128), 128)
        normed[at, :] = norm_into(grid_v[at, :], ggain_ref[...])
        return carry

    lax.fori_loop(0, points // 128, norm_block, 0)

    each_peer(lambda peer: need_to(peer, peer).wait_recv())
    lists = need_all[...]
    asked = jnp.broadcast_to(lists, (peers, cap, peers * cap))
    mine = iota((peers, cap, peers * cap), 2) == me * cap + iota((peers, cap, peers * cap), 1)
    wanted = jnp.sum(jnp.where(mine, asked.astype(F32), 0.0), axis=2, keepdims=True).astype(jnp.int32)
    wanted = wanted.reshape(peers * cap, 1)
    pick = jnp.where(wanted == iota((peers * cap, points), 1), 1.0, 0.0).astype(BF16)
    chosen = jnp.dot(pick, normed[...], preferred_element_type=F32).astype(BF16)
    def pass_query(peer):
        query_to(peer, peer).wait_recv()
        query_on(peer, peer).start()


    loads[2].wait()
    rows[...] = jnp.dot(chosen, wkv_v[...], preferred_element_type=F32).astype(BF16)

    each_chip(pass_query)
    each_peer(lambda peer: edges_to(peer, peer).wait_recv())
    mine = iota((cap, 128), 1) == lax.rem(me, group) * cap + iota((cap, 128), 0)
    entries = lax.dot_general(
        mine.astype(BF16), edges_all[...].reshape(peers * nodes, 128), NT, preferred_element_type=F32
    ).astype(BF16)
    fan = iota((peers * nodes, peers * lanes), 0)
    fan_lane = iota((peers * nodes, peers * lanes), 1)
    fan = fan == (fan_lane // lanes) * nodes + lax.rem(fan_lane, nodes)
    entries = jnp.dot(entries, jnp.where(fan, 1.0, 0.0).astype(BF16), preferred_element_type=F32)
    for peer in range(peers):
        times_all[peer] = entries[:, peer * lanes : (peer + 1) * lanes]

    own_head = iota((lanes, width), 0) // nodes == iota((lanes, width), 1) // head

    def window(w):
        spread_query = jnp.broadcast_to(query_all[w][None], (HEADS, nodes, width)).reshape(lanes, width)
        spread_query = jnp.where(own_head, spread_query, jnp.zeros_like(spread_query))
        here = pl.ds(pl.multiple_of(w * cap, cap), cap)
        scores = lax.dot_general(rows[here, :width], spread_query, NT, preferred_element_type=F32)
        times = times_all[w]
        scores = jnp.where(times > 0, scores * (1.0 / math.sqrt(head)), -1e30)
        highest = jnp.max(scores, axis=0, keepdims=True)
        raised = jnp.exp(scores - highest) * times
        total = jnp.sum(raised, axis=0, keepdims=True)
        mixed = lax.dot_general(raised.astype(BF16), rows[here, width:], TN, preferred_element_type=F32)
        mixed = jnp.where(own_head, mixed, 0.0).reshape(HEADS, nodes, width)
        return jnp.sum(mixed, axis=0).astype(BF16), highest, total

    def serve(windows):
        for peer, answer in [(peer, window(peer)) for peer in windows]:
            mix_send[peer] = answer[0]
            stat_send[peer, 0:1, :] = answer[1]
            stat_send[peer, 1:2, :] = answer[2]

    def reply(peer):
        mix_to(peer, me).start()
        stat_to(peer, me).start()

    serve([lax.rem(me + 2 * step, peers) for step in range(1, chips)])
    each_chip(reply)
    query_to(partner, partner).wait_recv()

    def take_passed(peer):
        owner = peer + 1 - 2 * side
        query_on(owner, owner).wait_recv()

    each_chip(take_passed)
    serve([lax.rem(partner + 2 * step, peers) for step in range(chips)])
    lax.fori_loop(0, chips, lambda step, carry: (reply(lax.rem(partner + 2 * step, peers)), carry)[1], 0)
    mixed, highest, total = window(me)
    mix_all[me] = mixed
    stat_all[me, 0:1, :] = highest
    stat_all[me, 1:2, :] = total

    loads[3].wait()
    queries_out[...] = jnp.dot(normed[...], wqd_v[...], preferred_element_type=F32).astype(BF16)
    queries_store = pltpu.make_async_copy(queries_out, queries_hbm, store_sem.at[0])
    queries_store.start()

    keys = peers * nodes
    dec_cap = table_ref.shape[0] * 128 // peers
    slots = dslot_ref[...]
    edge_total = slots.shape[0]
    slots = jnp.concatenate([slots] * (8 // edge_total), axis=0)
    columns = []
    for part in range(points // 128):
        piece = slots[:, part * 128 : (part + 1) * 128]
        high = piece // 128
        low = lax.rem(piece, 128)
        need = jnp.zeros_like(piece)
        for line in range(table_ref.shape[0]):
            entry = jnp.broadcast_to(table_ref[line : line + 1, :], piece.shape)
            need = jnp.where(high == line, jnp.take_along_axis(entry, low, axis=1), need)
        columns.append((piece // dec_cap) * nodes + need)
    node = jnp.concatenate(columns, axis=1)
    name = iota((keys, points), 0)
    times = jnp.zeros((keys, points), F32)
    for j in range(edge_total):
        times = times + jnp.where(node[j : j + 1, :] == name, 1.0, 0.0)
    bias_out[...] = jnp.where(times > 0, jnp.log(jnp.maximum(times, 1.0)), -1e30)
    bias_store = pltpu.make_async_copy(bias_out, bias_hbm, store_sem.at[1])
    bias_store.start()

    def take_mix(peer):
        mix_to(peer, peer).wait_recv()
        stat_to(peer, peer).wait_recv()

    each_peer(take_mix)
    tops = [stat_all[peer, 0:1, :] for peer in range(peers)]
    sums = [stat_all[peer, 1:2, :] for peer in range(peers)]
    top = functools.reduce(jnp.maximum, tops)
    shares = [jnp.exp(one - top) for one in tops]
    whole = functools.reduce(jnp.add, [a * b for a, b in zip(shares, sums)])
    own_node = iota((nodes, lanes), 0) == lax.rem(iota((nodes, lanes), 1), nodes)
    stacked = jnp.concatenate([jnp.where(own_node, share / whole, 0.0) for share in shares], axis=0)
    widen = (iota((lanes, width), 0) // nodes == iota((lanes, width), 1) // head).astype(F32)
    factors = jnp.dot(stacked, widen, precision=HIGH, preferred_element_type=F32).reshape(peers, nodes, width)
    enc_mixed = jnp.sum(factors * mix_all[...].astype(F32), axis=0).astype(BF16)
    loads[4].wait()
    update = jnp.dot(enc_mixed, wo_v[...], preferred_element_type=F32)
    fresh = (latent_ref[...].astype(F32) + update).astype(BF16)
    latent_out[...] = fresh
    loads[5].wait()
    pairs = jnp.dot(norm_into(fresh, dgain_ref[...]), wkvd_v[...], preferred_element_type=F32).astype(BF16)
    pairs_all[me] = pairs
    each_chip(lambda to: pairs_to(to, me).start())
    pairs_to(partner, me).start()

    def pass_pairs(peer):
        pairs_to(peer, peer).wait_recv()
        pairs_on(peer, peer).start()

    each_chip(pass_pairs)
    pairs_to(partner, partner).wait_recv()

    def take_pairs(peer):
        owner = peer + 1 - 2 * side
        pairs_on(owner, owner).wait_recv()

    each_chip(take_pairs)
    pairs_out[...] = pairs_all[...].reshape(peers * nodes, model)

    def drain(to):
        for outgoing in (need_to, edges_to, mix_to, stat_to):
            outgoing(to, me).wait_send()

    def drain_chip(to):
        query_to(to, me).wait_send()
        pairs_to(to, me).wait_send()
        query_on(to, to).wait_send()
        pairs_on(to, to).wait_send()

    queries_store.wait()
    bias_store.wait()
    each_peer(drain)
    each_chip(drain_chip)
    query_to(partner, me).wait_send()
    pairs_to(partner, me).wait_send()


def encode(grid, latent_in, grid_gain, node_gain, dec_gain, w_q_enc, w_kv_enc, w_o_enc, w_q_dec, w_kv_dec,
           enc_need, enc_slot, enc_count, dec_slot, dec_need):
    peers = lax.axis_size("dom")
    nodes, model = latent_in.shape
    width = w_q_enc.shape[1]
    entries = enc_need.shape[1]
    cap = entries // peers
    points = grid.shape[0]
    vmem = pl.BlockSpec(memory_space=pltpu.VMEM)
    far = pl.BlockSpec(memory_space=pl.ANY)
    return pl.pallas_call(
        functools.partial(encoder_kernel, peers),
        name="encode",
        out_shape=(
            jax.ShapeDtypeStruct((nodes, model), BF16),
            jax.ShapeDtypeStruct((peers * nodes, 2 * width), BF16),
            jax.ShapeDtypeStruct((points, width), BF16),
            jax.ShapeDtypeStruct((peers * nodes, points), F32),
        ),
        in_specs=[far, vmem, vmem, vmem, vmem, far, far, far, far, far, vmem, vmem, vmem, vmem, vmem],
        out_specs=(vmem, vmem, far, far),
        scratch_shapes=[
            pltpu.VMEM(grid.shape, BF16),
            pltpu.VMEM(w_q_enc.shape, BF16),
            pltpu.VMEM(w_kv_enc.shape, BF16),
            pltpu.VMEM(w_o_enc.shape, BF16),
            pltpu.VMEM(w_q_dec.shape, BF16),
            pltpu.VMEM(w_kv_dec.shape, BF16),
            pltpu.VMEM(grid.shape, BF16),
            pltpu.VMEM((entries, 2 * width), BF16),
            pltpu.VMEM((nodes, width), BF16),
            pltpu.VMEM((entries // 128, nodes, 128), BF16),
            pltpu.VMEM((peers, 1, entries), jnp.int32),
            pltpu.VMEM((peers, nodes, width), BF16),
            pltpu.VMEM((peers, nodes, 128), BF16),
            pltpu.VMEM((peers, cap, HEADS * nodes), F32),
            pltpu.VMEM((peers, nodes, width), BF16),
            pltpu.VMEM((peers, 2, HEADS * nodes), F32),
            pltpu.VMEM((peers, nodes, width), BF16),
            pltpu.VMEM((peers, 2, HEADS * nodes), F32),
            pltpu.VMEM((peers, nodes, 2 * width), BF16),
            pltpu.VMEM((points, width), BF16),
            pltpu.VMEM((peers * nodes, points), F32),
            pltpu.SemaphoreType.DMA((6,)),
            pltpu.SemaphoreType.DMA((2,)),
            pltpu.SemaphoreType.DMA((8, peers)),
            pltpu.SemaphoreType.DMA((8, peers)),
        ],
        compiler_params=pltpu.CompilerParams(
            collective_id=0, has_side_effects=True, vmem_limit_bytes=60 * 1024 * 1024
        ),
    )(grid, latent_in, grid_gain[None], node_gain[None], dec_gain[None], w_q_enc, w_kv_enc, w_o_enc, w_q_dec,
      w_kv_dec, enc_need, enc_slot.T, enc_count[None], dec_slot, dec_need.reshape(-1, 128))


def decoder_kernel(query_ref, pairs_ref, bias_ref, grid_hbm, wo_hbm, latent_ref, out_hbm, latent_out, keys_of, turned, mixed,
                   grid_v, wo_v, out_v, load_sem, store_sem):
    tile, width = query_ref.shape
    head = width // HEADS
    keys = pairs_ref.shape[0]
    quad = 4
    load_wo = pltpu.make_async_copy(wo_hbm, wo_v, load_sem.at[0])
    load_grid = pltpu.make_async_copy(grid_hbm, grid_v, load_sem.at[1])
    load_wo.start()
    load_grid.start()

    turned[...] = pairs_ref[:, width:].astype(F32).T.astype(BF16)
    latent_out[...] = latent_ref[...]
    lane_head = iota((keys, quad * head), 1) // head
    for h in range(HEADS):
        some = pairs_ref[:, (h // quad) * quad * head : (h // quad + 1) * quad * head] * (1.0 / math.sqrt(head))
        keys_of[h // quad, (h % quad) * keys : (h % quad + 1) * keys, :] = jnp.where(
            lane_head == h % quad, some, jnp.zeros_like(some)
        )

    for four in range(HEADS // quad):
        query = query_ref[:, four * quad * head : (four + 1) * quad * head]
        for side in range(quad):
            h = four * quad + side
            own = keys_of[four, side * keys : (side + 1) * keys, :]
            scores = lax.dot_general(own, query, NT, preferred_element_type=F32) + bias_ref[...]
            highest = jnp.max(scores, axis=0, keepdims=True)
            raised = jnp.exp(scores - highest)
            total = jnp.sum(raised, axis=0, keepdims=True)
            got = jnp.dot(turned[h * head : (h + 1) * head, :], raised.astype(BF16), preferred_element_type=F32)
            mixed[h * head : (h + 1) * head, :] = (got / total).astype(BF16)
    load_wo.wait()
    load_grid.wait()
    stores = []
    block = tile // 4
    for part in range(4):
        at = slice(part * block, (part + 1) * block)
        update = lax.dot_general(mixed[:, at], wo_v[...], TN, preferred_element_type=F32)
        out_v[at, :] = (grid_v[at, :].astype(F32) + update).astype(BF16)
        stores.append(pltpu.make_async_copy(out_v.at[at], out_hbm.at[at], store_sem.at[part]))
        stores[-1].start()
    for store in stores:
        store.wait()


def decode(queries, pairs, bias, grid, w_o_dec, latent_out):
    points, model = grid.shape
    width = queries.shape[1]
    tile = points
    vmem = pl.BlockSpec(memory_space=pltpu.VMEM)
    far = pl.BlockSpec(memory_space=pl.ANY)
    return pl.pallas_call(
        decoder_kernel,
        name="decode",
        out_shape=(
            jax.ShapeDtypeStruct(grid.shape, BF16),
            jax.ShapeDtypeStruct(latent_out.shape, BF16),
        ),
        in_specs=[vmem, vmem, vmem, far, far, vmem],
        out_specs=(far, vmem),
        scratch_shapes=[pltpu.VMEM((2, 4 * pairs.shape[0], width // 2), BF16), pltpu.VMEM((width, pairs.shape[0]), BF16), pltpu.VMEM((width, tile), BF16),
                        pltpu.VMEM(grid.shape, BF16), pltpu.VMEM(w_o_dec.shape, BF16), pltpu.VMEM(grid.shape, BF16),
                        pltpu.SemaphoreType.DMA((2,)), pltpu.SemaphoreType.DMA((4,))],
    )(queries, pairs, bias, grid, w_o_dec, latent_out)


def by_kernels(grid, latent_in, grid_gain, node_gain, dec_gain, w_q_enc, w_kv_enc, w_o_enc,
               w_q_dec, w_kv_dec, w_o_dec, enc_need, enc_slot, enc_count, dec_need, dec_slot):
    latent_out, pairs, queries, bias = encode(
        grid, latent_in, grid_gain, node_gain, dec_gain, w_q_enc, w_kv_enc, w_o_enc, w_q_dec, w_kv_dec,
        enc_need, enc_slot, enc_count, dec_slot, dec_need)
    grid_out, latent_out = decode(queries, pairs, bias, grid, w_o_dec, latent_out)
    return (latent_out, grid_out)


def chosen_form(*args):
    grid, latent_in, enc_need, dec_slot = args[0], args[1], args[11], args[15]
    peers = lax.axis_size("dom")
    cap = enc_need.shape[1] // peers
    small = latent_in.shape[0] * peers <= 256
    fits = peers % 2 == 0 and 128 % cap == 0 and cap % 32 == 0 and HEADS * latent_in.shape[0] == 128 and grid.shape[0] % 512 == 0
    if small and fits and 8 % dec_slot.shape[0] == 0:
        return by_kernels(*args)
    return on_device(*args)


def solution(mesh):
    both, rep = P(("groups", "dom"), None), P()
    return jax.shard_map(
        chosen_form,
        mesh=mesh,
        in_specs=(both, both, *([rep] * 9), P("dom", None), P(None, "dom"), P("dom"), P("dom", None), P(None, "dom")),
        out_specs=(both, both),
        check_vma=False,
    )
```
